256 devices in a mesh: row: 32 (over z, y), col: 8 (over x, core).
Axes of the slice: x: 4, y: 4, z: 8, core: 2. Of those that a mesh axis runs over, the one named last changes fastest.
Arguments:
- shot_dose: float32 [524288], P(('row', 'col')), may hold values from 0.25 to 4
- shot_owner: int32 [524288, 1], P(('row', 'col')), may hold values from 0 to 31; in each aligned block of 2048 rows (0 to 2047, 2048 to 4095, ...) at most 128 rows name the same one
- shot_cell: int32 [524288], P(('row', 'col')), may hold values from 0 to 15840
- shot_offset: int32 [524288], P(('row', 'col')), may hold values from 0 to 255
Outputs:
- final_dose: float32 [524288], P(('row', 'col'))
- backscatter_field: float32 [1024, 4096], P('row', 'col')
The draws below stay inside these ranges and needn't reach their ends.
Inputs may be any that keep to these rules, and one draw needn't show every extreme that they name: `shot_owner`: among the 2048 shots of one device at most 128 name the same tile row, and some tile row is named by exactly that many. `shot_cell`: A cell cy * 511 + cx with cy below 31 and cx below 511. `shot_offset`: oy * 16 + ox.
All inputs are finite; a program needn't handle non-finite values.
Results may differ from the reference program's by a relative error of at most 0.0001.
Values sent between devices are 32-bit elements; how exact they have to be, the bound alone decides.
No kernel may reach another device: no remote copies, remote signals or barrier semaphores. Data moves between devices by JAX's collectives and lax.ppermute only.
A program may use at most 64 MiB of HBM per device.

```python
import math
import jax
import jax.numpy as jnp
import numpy as np

CY = 32
CX = 512
S_DEV = 2048
HALF = 30
ITERS = 2
NYC = 1024
NXC = 4096
SHOTS = 524288
N_ROW = 32
N_COL = 8


def set_ends(drawn, key, least, high):
    spot = [jax.random.randint(jax.random.fold_in(key, axis), (), 0, length) for axis, length in enumerate(drawn.shape)]
    main_axis = drawn.shape.index(max(drawn.shape))
    neighbour = spot[:main_axis] + [(spot[main_axis] + 1) % drawn.shape[main_axis]] + spot[main_axis + 1:]
    return drawn.at[tuple(spot)].set(least).at[tuple(neighbour)].set(high)


def level_of(rng, shape, split, smallest, top_value):
    level, own = 1.0, jax.random.fold_in(rng, 6)
    for axis_at, parts in split:
        draws = jnp.exp(jax.random.uniform(jax.random.fold_in(own, axis_at), (parts,), jnp.float32, smallest / len(split), top_value / len(split)))
        level = level * jnp.repeat(draws, shape[axis_at] // parts).reshape([-1 if axis == axis_at else 1 for axis in range(len(shape))])
    return level


def assign_block(rng, own, number, rows, count, top, reach, skew):
    sequence = jax.random.permutation(rng, count)
    crowded, ordinary = load_shares(count, rows * top, reach, skew, True), load_shares(count, rows * top, reach, skew, False)
    places = jnp.arange(count)

    def named(lengths, offset_by):
        used = int((lengths > 0).sum())
        fixed = max(1, used // 4)
        moved = fixed + (places - fixed + offset_by * (used - fixed)) % max(1, count - fixed)
        return jnp.zeros((count,), jnp.int32).at[sequence[jnp.where(places < fixed, places, moved)]].set(jnp.asarray(lengths, jnp.int32))

    lengths = jnp.where(number % 4 == 0, named(crowded, number // 4), named(ordinary, number - number // 4 - 1))
    mixed = jax.random.permutation(jax.random.fold_in(own, 3), count)
    source_of, sink = mixed[0:count // 2 * 2:2], mixed[1:count // 2 * 2:2]
    slack = jnp.minimum(lengths[source_of] - 1, reach - lengths[sink]) // 2
    slack = jnp.where((source_of == sequence[0]) | (sink == sequence[0]) | (lengths[sink] == 0), 0, jnp.maximum(slack, 0))
    moved = jax.random.randint(jax.random.fold_in(own, 4), (count // 2,), 0, 1 << 20) % (slack + 1)
    lengths = lengths.at[source_of].add(-moved).at[sink].add(moved)
    members = jnp.searchsorted(jnp.cumsum(lengths), jnp.arange(rows * top), side="right").astype(jnp.int32)
    table = members.reshape(top, rows).T
    table = table[jax.random.permutation(jax.random.fold_in(own, 1), rows)]
    offset_by = jax.random.randint(jax.random.fold_in(own, 2), (rows, 1), 0, top)
    return jnp.take_along_axis(table, (jnp.arange(top)[None, :] + offset_by) % top, axis=1)


def load_shares(count, total, reach, slope, full):
    loads = [(1 << 20) // math.isqrt(rank ** slope) + 1 for rank in range(1, count + 1)]
    largest = reach if full else min(reach, max(-(-total // count), total * loads[0] // sum(loads)))
    least = 1 if total - largest >= count - 1 else 0
    counts, surplus = [largest] + [least] * (count - 1), total - largest - least * (count - 1)
    while surplus > 0:
        candidates = [i for i in range(1, count) if counts[i] < largest] or [i for i in range(1, count) if counts[i] < reach]
        pool, budget = sum([loads[i] for i in candidates]), surplus
        for i in candidates:
            extra = min(reach - counts[i], max(1, budget * loads[i] // pool), surplus)
            counts[i] = counts[i] + extra
            surplus = surplus - extra
    return np.array(counts)


def setup_inputs(seed: int = 0) -> dict:
    streams_of = jax.random.split(jax.random.key(seed), 5)
    shot_dose = jnp.clip(jnp.exp(math.log(4.0) - 2.7725887 * jax.random.uniform(streams_of[0], (SHOTS,), jnp.float32) ** level_of(streams_of[0], (SHOTS,), ((0, 256),), -0.2, 0.2)), 0.25, 4.0)
    shot_owner_keys = jax.random.split(jax.random.fold_in(streams_of[1], 1), SHOTS // S_DEV)
    shot_owner_turns = jax.random.permutation(jax.random.fold_in(streams_of[1], 3), SHOTS // S_DEV)
    shot_owner = jax.vmap(lambda own, number: assign_block(jax.random.fold_in(streams_of[1], 2), own, number, S_DEV, N_ROW, 1, 2 * S_DEV // N_ROW, 2))(shot_owner_keys, shot_owner_turns).reshape((SHOTS, 1))
    shot_cell = set_ends(jax.random.randint(streams_of[2], (SHOTS,), 0, (CY - 1) * (CX - 1)), jax.random.fold_in(streams_of[2], 1), 0, ((CY - 1) * (CX - 1)) - 1).astype(jnp.int32)
    shot_offset = set_ends(jax.random.randint(streams_of[3], (SHOTS,), 0, 256), jax.random.fold_in(streams_of[3], 1), 0, 255).astype(jnp.int32)
    return {"shot_dose": shot_dose, "shot_owner": shot_owner, "shot_cell": shot_cell, "shot_offset": shot_offset}


backscatter_ratio = 0.6
kernel_spread = 10.0


def kernel_taps():
    lags = jnp.arange(2 * HALF + 1).astype(jnp.float32) - HALF
    values = jnp.exp(-(lags * lags) / (2.0 * kernel_spread * kernel_spread))
    return values / jnp.sum(values)


def blurred(density):
    taps = kernel_taps()
    padded = jnp.pad(density, ((HALF, HALF), (0, 0)))
    along_y = jnp.zeros_like(density)
    for tap_index in range(2 * HALF + 1):
        along_y = along_y + taps[tap_index] * padded[tap_index:tap_index + NYC, :]
    padded = jnp.pad(along_y, ((0, 0), (HALF, HALF)))
    along_x = jnp.zeros_like(density)
    for tap_index in range(2 * HALF + 1):
        along_x = along_x + taps[tap_index] * padded[:, tap_index:tap_index + NXC]
    return along_x


def reference(shot_dose, shot_owner, shot_cell, shot_offset):
    device_of = (jnp.arange(SHOTS) // S_DEV).astype(jnp.int32)
    column_of = device_of % N_COL
    owners = shot_owner[:, 0]
    glob_row = owners * CY + shot_cell // (CX - 1)
    glob_col = column_of * CX + shot_cell % (CX - 1)
    base_cell = glob_row * NXC + glob_col
    corners = jnp.stack([base_cell, base_cell + 1, base_cell + NXC, base_cell + NXC + 1]).astype(jnp.int32)
    off_row = (shot_offset // 16).astype(jnp.float32)
    off_col = (shot_offset % 16).astype(jnp.float32)
    weights = jnp.stack([(16.0 - off_row) * (16.0 - off_col), (16.0 - off_row) * off_col,
                         off_row * (16.0 - off_col), off_row * off_col]) / 256.0
    dose_now = shot_dose
    field_now = jnp.zeros((NYC, NXC), jnp.float32)
    for iteration in range(ITERS):
        flat_density = jnp.zeros((NYC * NXC,), jnp.float32).at[corners.reshape(-1)].add(
            (weights * dose_now[None, :]).reshape(-1))
        density = flat_density.reshape(NYC, NXC)
        field_now = blurred(density)
        total_field = (density + backscatter_ratio * field_now).reshape(-1)
        exposure = jnp.sum(weights * total_field[corners], axis=0)
        dose_now = dose_now * (1.0 + backscatter_ratio) / exposure
    return dose_now, field_now
```

```python
import jax
import jax.numpy as jnp
import numpy as np
from jax import lax
from jax.experimental import pallas as pl
from jax.experimental.pallas import tpu as pltpu
from jax.sharding import PartitionSpec as P

CY = 32
CX = 512
HALF = 30
N_ROW = 32
N_COL = 8
S_DEV = 2048
CAP = 128
REACH = 2
NT = 2 * REACH + 1
BLK = 128
NB = CX // BLK
XR = BLK + 16
SLOTS = N_ROW * CAP
BF = jnp.bfloat16
F32 = jnp.float32

BACKSCATTER = 0.6
SPREAD = 10.0


def taps():
    lags = np.arange(2 * HALF + 1, dtype=np.float64) - HALF
    values = np.exp(-(lags * lags) / (2.0 * SPREAD * SPREAD))
    return values / values.sum()


def band(rows, cols, offset):
    lag = np.arange(cols)[None, :] - np.arange(rows)[:, None] - offset + HALF
    t = taps()
    return np.where((lag >= 0) & (lag <= 2 * HALF), t[np.clip(lag, 0, 2 * HALF)], 0.0)


def two(m):
    hi = m.astype(jnp.bfloat16)
    lo = (m - hi.astype(np.float64)).astype(jnp.bfloat16)
    return np.asarray(hi), np.asarray(lo)


def left_constant(rows, cols, offset):
    hi, lo = two(band(rows, cols, offset))
    return np.concatenate([np.concatenate([hi, hi], 1), np.concatenate([lo, lo], 1)], 0)


def right_constant():
    hi, lo = two(band(BLK, 3 * BLK, BLK).T)
    return np.concatenate([hi, lo], 1)


def split2(v):
    hi = v.astype(BF)
    lo = (v - hi.astype(F32)).astype(BF)
    return hi, lo


def split3(v):
    hi = v.astype(BF).astype(F32)
    rest = v - hi
    mid = rest.astype(BF).astype(F32)
    return hi, mid, rest - mid


def nt_dot(a, b):
    return lax.dot_general(a, b, (((1,), (1,)), ((), ())), preferred_element_type=F32)


def nn_dot(a, b):
    return lax.dot_general(a, b, (((1,), (0,)), ((), ())), preferred_element_type=F32)


def shifted_rows(v, by):
    if by == 0:
        return v
    pad = jnp.zeros((abs(by), v.shape[1]), v.dtype)
    return jnp.concatenate([v[by:], pad], 0) if by > 0 else jnp.concatenate([pad, v[:by]], 0)


def pack_kernel(dose_ref, owner_ref, cell_ref, offset_ref, send_ref, rank_ref):
    owner = owner_ref[...]
    place = (cell_ref[...] * 256 + offset_ref[...]).astype(F32)
    dose = dose_ref[...]
    chunk = 256
    n_chunks = S_DEV // chunk
    mine = owner == lax.broadcasted_iota(jnp.int32, (N_ROW, S_DEV), 0)
    ones = jnp.where(mine, 1.0, 0.0)
    stacked = jnp.concatenate([ones[:, c * chunk:(c + 1) * chunk] for c in range(n_chunks)], 0).astype(BF)
    rows_at = lax.broadcasted_iota(jnp.int32, (chunk, chunk), 0)
    cols_at = lax.broadcasted_iota(jnp.int32, (chunk, chunk), 1)
    before = jnp.where(rows_at < cols_at, 1.0, 0.0).astype(BF)
    prefix = nn_dot(stacked, before)
    totals = nn_dot(stacked, jnp.ones((chunk, chunk), BF))
    base = jnp.zeros((N_ROW, chunk), F32)
    ranks = []
    for c in range(n_chunks):
        here = slice(c * N_ROW, (c + 1) * N_ROW)
        inside = ones[:, c * chunk:(c + 1) * chunk]
        ranks.append(jnp.sum(inside * (prefix[here] + base), axis=0, keepdims=True))
        base = base + totals[here]
    rank = jnp.concatenate(ranks, 1)
    rank_ref[...] = rank
    at_rank = jnp.where(rank == lax.broadcasted_iota(jnp.int32, (CAP, S_DEV), 0).astype(F32), 1.0, 0.0).astype(BF)
    parts = [jnp.where(mine, part, 0.0).astype(BF) for part in split3(place) + split3(dose)]
    packed = nt_dot(jnp.concatenate(parts, 0), at_rank)
    for which in range(2):
        p = packed[3 * which * N_ROW:3 * (which + 1) * N_ROW]
        whole = p[:N_ROW] + p[N_ROW:2 * N_ROW] + p[2 * N_ROW:]
        for t in range(NT):
            start = (2 * t + which) * CAP
            send_ref[:, 0, start:start + CAP] = shifted_rows(whole, t - REACH)


def decoded(place):
    cell = jnp.floor(place * (1.0 / 256.0))
    fine = place - 256.0 * cell
    cell_y = jnp.floor((cell + 0.5) * (1.0 / (CX - 1)))
    cell_x = cell - (CX - 1) * cell_y
    off_y = jnp.floor(fine * (1.0 / 16.0))
    off_x = fine - 16.0 * off_y
    block = jnp.floor(cell_x * (1.0 / BLK))
    return block, cell_y, cell_x - BLK * block, off_y * (1.0 / 16.0), off_x * (1.0 / 16.0)


def over_rows(v, rows):
    return jnp.broadcast_to(v, (rows, v.shape[1])).astype(BF)


def build_columns(column, off_x, b_ref, rows0):
    for i in range(N_ROW):
        here = slice(i * CAP, (i + 1) * CAP)
        at = lax.broadcasted_iota(jnp.int32, (XR, CAP), 0).astype(F32).astype(BF)
        first = over_rows(column[i:i + 1], XR)
        second = over_rows(column[i:i + 1] + 1.0, XR)
        w0 = over_rows(1.0 - off_x[i:i + 1], XR)
        w1 = over_rows(off_x[i:i + 1], XR)
        b_ref[rows0:rows0 + XR, here] = jnp.where(at == first, w0, jnp.where(at == second, w1, jnp.zeros_like(w0)))


def build_rows(key, off_y, dose, a_ref):
    hi0, lo0 = split2((1.0 - off_y) * dose)
    hi1, lo1 = split2(off_y * dose)
    hi0, lo0, hi1, lo1 = (v.astype(F32) for v in (hi0, lo0, hi1, lo1))
    for i in range(N_ROW):
        here = slice(i * CAP, (i + 1) * CAP)
        at = lax.broadcasted_iota(jnp.int32, (BLK, CAP), 0).astype(F32).astype(BF)
        first = at == over_rows(key[i:i + 1], BLK)
        second = at == over_rows(key[i:i + 1] + 1.0, BLK)
        for part, (p0, p1) in enumerate(((hi0, hi1), (lo0, lo1))):
            q0, q1 = over_rows(p0[i:i + 1], BLK), over_rows(p1[i:i + 1], BLK)
            a_ref[part * BLK:(part + 1) * BLK, here] = jnp.where(first, q0, jnp.where(second, q1, jnp.zeros_like(q0)))


def tile_density(a, b):
    both = nt_dot(a, b)
    d = both[:BLK] + both[BLK:]
    blocks = [d[:CY, :BLK]]
    for h in range(1, NB):
        over = d[(h - 1) * CY:h * CY, BLK:XR]
        over = jnp.concatenate([over, jnp.zeros((CY, BLK - XR + BLK), F32)], 1)
        blocks.append(d[h * CY:(h + 1) * CY, :BLK] + over)
    return jnp.concatenate(blocks, 1)


def packed_edge(block, lane0):
    rows = block.shape[0] // 4
    lane = lax.broadcasted_iota(jnp.int32, (rows, BLK), 1)
    out = jnp.zeros((rows, BLK), block.dtype)
    for g in range(4):
        part = block[g * rows:(g + 1) * rows]
        shift = (32 * g - lane0) % BLK
        part = pltpu.roll(part, shift, 1) if shift else part
        out = jnp.where(lane // 32 == g, part, out)
    return out


def unpacked_edge(edge, lane0):
    parts = []
    for g in range(4):
        shift = (lane0 - 32 * g) % BLK
        parts.append(pltpu.roll(edge, shift, 1) if shift else edge)
    return jnp.concatenate(parts, 0)


def blurred_y(density, taps_ref):
    hi, lo = split2(density)
    both = nn_dot(taps_ref[...], jnp.concatenate([hi, lo], 0))
    rows = both.shape[0] // 2
    return both[:rows] + both[rows:]


def blurred_x(along_y, left, right, taps_ref):
    wide = jnp.concatenate([left, along_y, right], 1)
    rows = along_y.shape[0]
    stacked = jnp.concatenate([wide[:, h * BLK:(h + 3) * BLK] for h in range(NB)], 0)
    hi, lo = split2(stacked)
    both = nn_dot(jnp.concatenate([hi, lo], 0), taps_ref[...])
    both = both[:NB * rows] + both[NB * rows:]
    out = both[:, :BLK] + both[:, BLK:]
    return jnp.concatenate([out[h * rows:(h + 1) * rows] for h in range(NB)], 1)


def gathered(total, key_block, cell_y, off_y, b):
    pieces = []
    for h in range(NB):
        inside = total[:, h * BLK:(h + 1) * BLK]
        if h + 1 < NB:
            after = total[:, (h + 1) * BLK:(h + 1) * BLK + XR - BLK]
        else:
            after = jnp.zeros((CY, XR - BLK), F32)
        pieces.append(jnp.concatenate([inside, after], 1))
    hi, lo = split2(jnp.concatenate(pieces, 0))
    both = nn_dot(jnp.concatenate([hi, lo], 0), b)
    at = lax.broadcasted_iota(jnp.int32, (CY, CAP), 0).astype(F32)
    rows = []
    for i in range(N_ROW):
        here = slice(i * CAP, (i + 1) * CAP)
        g = both[:BLK, here] + both[BLK:, here]
        block = key_block[i:i + 1]
        mine = g[:CY]
        for h in range(1, NB):
            mine = jnp.where(block == float(h), g[h * CY:(h + 1) * CY], mine)
        y, o = cell_y[i:i + 1], off_y[i:i + 1]
        w = jnp.where(at == y, 1.0 - o, jnp.where(at == y + 1.0, o, 0.0))
        rows.append(jnp.sum(w * mine, axis=0, keepdims=True))
    return jnp.concatenate(rows, 0)


def corrected(dose, exposure):
    return jnp.where(dose > 0.0, dose * (1.0 + BACKSCATTER) / exposure, 0.0)


def first_kernel(recv_ref, ltaps_ref, along_ref, density_ref, to_left_ref, to_right_ref, a_ref, b_ref):
    tiles = []
    for t in range(NT):
        place = recv_ref[:, 0, 2 * t * CAP:(2 * t + 1) * CAP]
        dose = recv_ref[:, 0, (2 * t + 1) * CAP:(2 * t + 2) * CAP]
        block, cell_y, column, off_y, off_x = decoded(place)
        build_columns(column, off_x, b_ref, 0)
        build_rows(block * CY + cell_y, off_y, dose, a_ref)
        tiles.append(tile_density(a_ref[...], b_ref[...]))
    density_ref[...] = jnp.concatenate(tiles[1:NT - 1], 0)
    along = blurred_y(jnp.concatenate(tiles, 0), ltaps_ref)
    along_ref[...] = along
    to_left_ref[...] = packed_edge(along[:, :BLK], 0)
    to_right_ref[...] = packed_edge(along[:, CX - BLK:], BLK - 32)


def second_kernel(sides_ref, recv_ref, along_ref, density_ref, from_left_ref, from_right_ref, rtaps_ref, ltaps_ref,
                  dose_ref, along2_ref, density2_ref, to_left_ref, to_right_ref, a_ref, b_ref):
    left = unpacked_edge(from_left_ref[...] * sides_ref[0], BLK - 32)
    right = unpacked_edge(from_right_ref[...] * sides_ref[1], 0)
    field = blurred_x(along_ref[...], left, right, rtaps_ref)
    total = density_ref[...] + BACKSCATTER * field
    tiles = []
    for n in range(NT - 2):
        t = n + 1
        place = recv_ref[:, 0, 2 * t * CAP:(2 * t + 1) * CAP]
        dose = recv_ref[:, 0, (2 * t + 1) * CAP:(2 * t + 2) * CAP]
        block, cell_y, column, off_y, off_x = decoded(place)
        build_columns(column, off_x, b_ref, 0)
        exposure = gathered(total[n * CY:(n + 1) * CY], block, cell_y, off_y, b_ref[...])
        dose = corrected(dose, exposure)
        if t == REACH:
            dose_ref[...] = dose
        build_rows(block * CY + cell_y, off_y, dose, a_ref)
        tiles.append(tile_density(a_ref[...], b_ref[...]))
    density2_ref[...] = tiles[1]
    along = blurred_y(jnp.concatenate(tiles, 0), ltaps_ref)
    along2_ref[...] = along
    to_left_ref[...] = packed_edge(along[:, :BLK], 0)
    to_right_ref[...] = packed_edge(along[:, CX - BLK:], BLK - 32)


def third_kernel(sides_ref, recv_ref, dose_ref, along_ref, density_ref, from_left_ref, from_right_ref, rtaps_ref,
                 field_ref, final_ref, b_ref):
    left = unpacked_edge(from_left_ref[...] * sides_ref[0], BLK - 32)
    right = unpacked_edge(from_right_ref[...] * sides_ref[1], 0)
    field = blurred_x(along_ref[...], left, right, rtaps_ref)
    field_ref[...] = field
    total = density_ref[...] + BACKSCATTER * field
    place = recv_ref[:, 0, 2 * REACH * CAP:(2 * REACH + 1) * CAP]
    block, cell_y, column, off_y, off_x = decoded(place)
    build_columns(column, off_x, b_ref, 0)
    exposure = gathered(total, block, cell_y, off_y, b_ref[...])
    final_ref[:, 0, :] = corrected(dose_ref[...], exposure)


def unpack_kernel(ret_ref, owner_ref, rank_ref, out_ref):
    mine = owner_ref[...] == lax.broadcasted_iota(jnp.int32, (N_ROW, S_DEV), 0)
    at_rank = jnp.where(rank_ref[...] == lax.broadcasted_iota(jnp.int32, (CAP, S_DEV), 0).astype(F32), 1.0, 0.0).astype(BF)
    parts = jnp.concatenate([p.astype(BF) for p in split3(ret_ref[:, 0, :])], 0)
    g = nn_dot(parts, at_rank)
    whole = g[:N_ROW] + g[N_ROW:2 * N_ROW] + g[2 * N_ROW:]
    out_ref[...] = jnp.sum(jnp.where(mine, whole, 0.0), axis=0, keepdims=True)


def vmem():
    return pl.BlockSpec(memory_space=pltpu.VMEM)


def call(kernel, outs, n_in, scratch=(), scalars=0):
    return pl.pallas_call(
        kernel,
        out_shape=[jax.ShapeDtypeStruct(s, F32) for s in outs],
        in_specs=[pl.BlockSpec(memory_space=pltpu.SMEM)] * scalars + [vmem()] * (n_in - scalars),
        out_specs=[vmem() for _ in outs],
        scratch_shapes=list(scratch),
        compiler_params=pltpu.CompilerParams(vmem_limit_bytes=48 << 20),
    )


def exchanged(to_left, to_right):
    n = lax.axis_size("col")
    from_left = lax.ppermute(to_right, "col", [(i, (i + 1) % n) for i in range(n)])
    from_right = lax.ppermute(to_left, "col", [((i + 1) % n, i) for i in range(n)])
    return from_left, from_right


def per_device(shot_dose, shot_owner, shot_cell, shot_offset):
    col = lax.axis_index("col")
    sides = jnp.stack([col > 0, col < N_COL - 1]).astype(F32)
    owner = shot_owner.reshape(1, S_DEV)
    ltaps = jnp.asarray(left_constant(3 * CY, NT * CY, CY))
    ltaps2 = jnp.asarray(left_constant(CY, 3 * CY, CY))
    rtaps = jnp.asarray(right_constant())
    send, rank = call(pack_kernel, [(N_ROW, 1, 2 * NT * CAP), (1, S_DEV)], 4)(
        shot_dose.reshape(1, S_DEV), owner, shot_cell.reshape(1, S_DEV), shot_offset.reshape(1, S_DEV)
    )
    recv = lax.all_to_all(send, "row", split_axis=0, concat_axis=0, tiled=True)
    a_scratch, b_scratch = pltpu.VMEM((2 * BLK, SLOTS), BF), pltpu.VMEM((XR, SLOTS), BF)
    edge = (3 * CY // 4, BLK)
    along, density, to_left, to_right = call(
        first_kernel, [(3 * CY, CX), (3 * CY, CX), edge, edge], 2, (a_scratch, b_scratch)
    )(recv, ltaps)
    from_left, from_right = exchanged(to_left, to_right)
    edge = (CY // 4, BLK)
    dose, along, density, to_left, to_right = call(
        second_kernel, [(N_ROW, CAP), (CY, CX), (CY, CX), edge, edge], 8, (a_scratch, b_scratch), 1
    )(sides, recv, along, density, from_left, from_right, rtaps, ltaps2)
    from_left, from_right = exchanged(to_left, to_right)
    field, final = call(third_kernel, [(CY, CX), (N_ROW, 1, CAP)], 8, (b_scratch,), 1)(
        sides, recv, dose, along, density, from_left, from_right, rtaps
    )
    back = lax.all_to_all(final, "row", split_axis=0, concat_axis=0, tiled=True)
    (out,) = call(unpack_kernel, [(1, S_DEV)], 3)(back, owner, rank)
    return out.reshape(S_DEV), field


def solution(mesh):
    placed = (P(("row", "col")), P(("row", "col"), None), P(("row", "col")), P(("row", "col")))
    return jax.shard_map(
        per_device,
        mesh=mesh,
        in_specs=placed,
        out_specs=(P(("row", "col")), P("row", "col")),
        check_vma=False,
    )
```

```python
import jax
import jax.numpy as jnp
import numpy as np
from jax import lax
from jax.experimental import pallas as pl
from jax.experimental.pallas import tpu as pltpu
from jax.sharding import PartitionSpec as P

CY = 32
CX = 512
HALF = 30
N_ROW = 32
N_COL = 8
S_DEV = 2048
CAP = 128
REACH = 2
NT = 2 * REACH + 1
BLK = 128
NB = CX // BLK
XR = BLK + 16
SLOTS = N_ROW * CAP
SUB16 = 16
BF = jnp.bfloat16
F32 = jnp.float32

BACKSCATTER = 0.6
SPREAD = 10.0


def taps():
    lags = np.arange(2 * HALF + 1, dtype=np.float64) - HALF
    values = np.exp(-(lags * lags) / (2.0 * SPREAD * SPREAD))
    return values / values.sum()


def band(rows, cols, offset):
    lag = np.arange(cols)[None, :] - np.arange(rows)[:, None] - offset + HALF
    t = taps()
    return np.where((lag >= 0) & (lag <= 2 * HALF), t[np.clip(lag, 0, 2 * HALF)], 0.0)


def two(m):
    hi = m.astype(jnp.bfloat16)
    lo = (m - hi.astype(np.float64)).astype(jnp.bfloat16)
    return np.asarray(hi), np.asarray(lo)


def left_constant(rows, cols, offset):
    hi, lo = two(band(rows, cols, offset))
    return np.concatenate([np.concatenate([hi, hi], 1), np.concatenate([lo, lo], 1)], 0)


def right_constant():
    hi, lo = two(band(BLK, 3 * BLK, BLK).T)
    return np.concatenate([hi, lo], 1)


def split2(v):
    hi = v.astype(BF)
    lo = (v - hi.astype(F32)).astype(BF)
    return hi, lo


def split3(v):
    hi = v.astype(BF).astype(F32)
    rest = v - hi
    mid = rest.astype(BF).astype(F32)
    return hi, mid, rest - mid


def nt_dot(a, b):
    return lax.dot_general(a, b, (((1,), (1,)), ((), ())), preferred_element_type=F32)


def nn_dot(a, b):
    return lax.dot_general(a, b, (((1,), (0,)), ((), ())), preferred_element_type=F32)


def shifted_rows(v, by):
    if by == 0:
        return v
    pad = jnp.zeros((abs(by), v.shape[1]), v.dtype)
    return jnp.concatenate([v[by:], pad], 0) if by > 0 else jnp.concatenate([pad, v[:by]], 0)


def pack_kernel(dose_ref, owner_ref, cell_ref, offset_ref, send_ref, rank_ref):
    owner = owner_ref[...]
    place = (cell_ref[...] * 256 + offset_ref[...]).astype(F32)
    dose = dose_ref[...]
    chunk = 256
    n_chunks = S_DEV // chunk
    mine = owner == lax.broadcasted_iota(jnp.int32, (N_ROW, S_DEV), 0)
    ones = jnp.where(mine, 1.0, 0.0)
    stacked = jnp.concatenate([ones[:, c * chunk:(c + 1) * chunk] for c in range(n_chunks)], 0).astype(BF)
    rows_at = lax.broadcasted_iota(jnp.int32, (chunk, chunk), 0)
    cols_at = lax.broadcasted_iota(jnp.int32, (chunk, chunk), 1)
    before = jnp.where(rows_at < cols_at, 1.0, 0.0).astype(BF)
    prefix = nn_dot(stacked, before)
    totals = nn_dot(stacked, jnp.ones((chunk, chunk), BF))
    base = jnp.zeros((N_ROW, chunk), F32)
    ranks = []
    for c in range(n_chunks):
        here = slice(c * N_ROW, (c + 1) * N_ROW)
        inside = ones[:, c * chunk:(c + 1) * chunk]
        ranks.append(jnp.sum(inside * (prefix[here] + base), axis=0, keepdims=True))
        base = base + totals[here]
    rank = jnp.concatenate(ranks, 1)
    rank_ref[...] = rank
    at_rank = jnp.where(rank == lax.broadcasted_iota(jnp.int32, (CAP, S_DEV), 0).astype(F32), 1.0, 0.0).astype(BF)
    parts = [jnp.where(mine, part, 0.0).astype(BF) for part in split3(place) + split3(dose)]
    packed = nt_dot(jnp.concatenate(parts, 0), at_rank)
    for which in range(2):
        p = packed[3 * which * N_ROW:3 * (which + 1) * N_ROW]
        whole = p[:N_ROW] + p[N_ROW:2 * N_ROW] + p[2 * N_ROW:]
        for t in range(NT):
            start = (2 * t + which) * CAP
            send_ref[:, 0, start:start + CAP] = shifted_rows(whole, t - REACH)


def decoded(place):
    cell = jnp.floor(place * (1.0 / 256.0))
    fine = place - 256.0 * cell
    cell_y = jnp.floor((cell + 0.5) * (1.0 / (CX - 1)))
    cell_x = cell - (CX - 1) * cell_y
    off_y = jnp.floor(fine * (1.0 / 16.0))
    off_x = fine - 16.0 * off_y
    block = jnp.floor(cell_x * (1.0 / BLK))
    column = cell_x - BLK * block
    off_y, off_x = off_y * (1.0 / 16.0), off_x * (1.0 / 16.0)
    return dict(block=block, y=cell_y, y1=cell_y + 1.0, column=column, column1=column + 1.0,
                y0w=1.0 - off_y, y1w=off_y, x0=1.0 - off_x, x1=off_x)


def pair_columns(shot):
    return lambda i: jnp.concatenate([column_chunk(shot, i), column_chunk(shot, i + 1)], 1)


def over_rows(v, i):
    return jnp.broadcast_to(v[i:i + 1], (SUB16, CAP)).astype(BF)


def row_numbers(first):
    return (lax.broadcasted_iota(jnp.int32, (SUB16, CAP), 0) + first).astype(F32).astype(BF)


def column_chunk(shot, i):
    first, second = over_rows(shot["column"], i), over_rows(shot["column1"], i)
    w0, w1 = over_rows(shot["x0"], i), over_rows(shot["x1"], i)
    none = jnp.zeros_like(w0)
    out = []
    for k in range(XR // SUB16):
        at = row_numbers(SUB16 * k)
        out.append(jnp.where(at == first, w0, jnp.where(at == second, w1, none)))
    return jnp.concatenate(out, 0)


def row_chunk(shot, dosed, i):
    first, second = over_rows(shot["y"], i), over_rows(shot["y1"], i)
    block = over_rows(shot["block"], i)
    values = [over_rows(v, i) for v in dosed]
    none = jnp.zeros_like(first)
    parts = [[], []]
    for k in range(CY // SUB16):
        at = row_numbers(SUB16 * k)
        on_first, on_second = at == first, at == second
        for part in range(2):
            q0, q1 = values[2 * part:2 * part + 2]
            parts[part].append(jnp.where(on_first, q0, jnp.where(on_second, q1, none)))
    inside = [block == jnp.full((SUB16, CAP), h, F32).astype(BF) for h in range(NB)]
    return jnp.concatenate([jnp.where(inside[h], v, none) for part in parts for h in range(NB) for v in part], 0)


def dosed_weights(shot, dose):
    hi0, lo0 = split2(shot["y0w"] * dose)
    hi1, lo1 = split2(shot["y1w"] * dose)
    return [v.astype(F32) for v in (hi0, hi1, lo0, lo1)]


def tile_density(shot, dose, columns):
    dosed = dosed_weights(shot, dose)
    both = None
    for i in range(0, N_ROW, 2):
        a = jnp.concatenate([row_chunk(shot, dosed, i), row_chunk(shot, dosed, i + 1)], 1)
        one = nt_dot(a, columns(i))
        both = one if both is None else both + one
    d = both[:BLK] + both[BLK:]
    blocks = [d[:CY, :BLK]]
    for h in range(1, NB):
        over = d[(h - 1) * CY:h * CY, BLK:XR]
        over = jnp.concatenate([over, jnp.zeros((CY, BLK - XR + BLK), F32)], 1)
        blocks.append(d[h * CY:(h + 1) * CY, :BLK] + over)
    return jnp.concatenate(blocks, 1)


def packed_edge(block, lane0):
    rows = block.shape[0] // 4
    lane = lax.broadcasted_iota(jnp.int32, (rows, BLK), 1)
    out = jnp.zeros((rows, BLK), block.dtype)
    for g in range(4):
        part = block[g * rows:(g + 1) * rows]
        shift = (32 * g - lane0) % BLK
        part = pltpu.roll(part, shift, 1) if shift else part
        out = jnp.where(lane // 32 == g, part, out)
    return out


def unpacked_edge(edge, lane0):
    parts = []
    for g in range(4):
        shift = (lane0 - 32 * g) % BLK
        parts.append(pltpu.roll(edge, shift, 1) if shift else edge)
    return jnp.concatenate(parts, 0)


def blurred_y(density, taps_ref):
    hi, lo = split2(density)
    both = nn_dot(taps_ref[...], jnp.concatenate([hi, lo], 0))
    rows = both.shape[0] // 2
    return both[:rows] + both[rows:]


def blurred_x(along_y, left, right, taps_ref):
    wide = jnp.concatenate([left, along_y, right], 1)
    rows = along_y.shape[0]
    stacked = jnp.concatenate([wide[:, h * BLK:(h + 3) * BLK] for h in range(NB)], 0)
    hi, lo = split2(stacked)
    both = nn_dot(jnp.concatenate([hi, lo], 0), taps_ref[...])
    both = both[:NB * rows] + both[NB * rows:]
    out = both[:, :BLK] + both[:, BLK:]
    return jnp.concatenate([out[h * rows:(h + 1) * rows] for h in range(NB)], 1)


def gathered(total, shot, b_ref):
    pieces = []
    for h in range(NB):
        inside = total[:, h * BLK:(h + 1) * BLK]
        if h + 1 < NB:
            after = total[:, (h + 1) * BLK:(h + 1) * BLK + XR - BLK]
        else:
            after = jnp.zeros((CY, XR - BLK), F32)
        pieces.append(jnp.concatenate([inside, after], 1))
    hi, lo = split2(jnp.concatenate(pieces, 0))
    table = jnp.concatenate([hi, lo], 0)
    at = lax.broadcasted_iota(jnp.int32, (CY, CAP), 0).astype(F32)
    rows = []
    for i in range(0, N_ROW, 2):
        columns = pair_columns(shot)(i)
        if b_ref is not None:
            b_ref[:, i * CAP:(i + 2) * CAP] = columns
        both = nn_dot(table, columns)
        for j in range(2):
            here = slice(j * CAP, (j + 1) * CAP)
            g = both[:BLK, here] + both[BLK:, here]
            block = shot["block"][i + j:i + j + 1]
            mine = g[:CY]
            for h in range(1, NB):
                mine = jnp.where(block == float(h), g[h * CY:(h + 1) * CY], mine)
            y, y1 = shot["y"][i + j:i + j + 1], shot["y1"][i + j:i + j + 1]
            w = jnp.where(at == y, shot["y0w"][i + j:i + j + 1], jnp.where(at == y1, shot["y1w"][i + j:i + j + 1], 0.0))
            rows.append(jnp.sum(w * mine, axis=0, keepdims=True))
    return jnp.concatenate(rows, 0)


def corrected(dose, exposure):
    return jnp.where(dose > 0.0, dose * (1.0 + BACKSCATTER) / exposure, 0.0)


def slots(recv_ref, t):
    start = 2 * t * CAP
    return recv_ref[:, 0, start:start + CAP], recv_ref[:, 0, start + CAP:start + 2 * CAP]


def first_kernel(recv_ref, ltaps_ref, along_ref, density_ref, to_left_ref, to_right_ref):
    tiles = []
    for t in range(NT):
        place, dose = slots(recv_ref, t)
        shot = decoded(place)
        tiles.append(tile_density(shot, dose, pair_columns(shot)))
    density_ref[...] = jnp.concatenate(tiles[1:NT - 1], 0)
    along = blurred_y(jnp.concatenate(tiles, 0), ltaps_ref)
    along_ref[...] = along
    to_left_ref[...] = packed_edge(along[:, :BLK], 0)
    to_right_ref[...] = packed_edge(along[:, CX - BLK:], BLK - 32)


def field_of(along_ref, from_left_ref, from_right_ref, rtaps_ref):
    col = lax.axis_index("col")
    left = unpacked_edge(jnp.where(col > 0, from_left_ref[...], 0.0), BLK - 32)
    right = unpacked_edge(jnp.where(col < N_COL - 1, from_right_ref[...], 0.0), 0)
    return blurred_x(along_ref[...], left, right, rtaps_ref)


def second_kernel(recv_ref, along_ref, density_ref, from_left_ref, from_right_ref, rtaps_ref, ltaps_ref,
                  dose_ref, along2_ref, density2_ref, to_left_ref, to_right_ref, b_ref):
    total = density_ref[...] + BACKSCATTER * field_of(along_ref, from_left_ref, from_right_ref, rtaps_ref)
    tiles = []
    for n in range(NT - 2):
        place, dose = slots(recv_ref, n + 1)
        shot = decoded(place)
        exposure = gathered(total[n * CY:(n + 1) * CY], shot, b_ref)
        dose = corrected(dose, exposure)
        if n + 1 == REACH:
            dose_ref[...] = dose
        tiles.append(tile_density(shot, dose, lambda i: b_ref[:, i * CAP:(i + 2) * CAP]))
    density2_ref[...] = tiles[1]
    along = blurred_y(jnp.concatenate(tiles, 0), ltaps_ref)
    along2_ref[...] = along
    to_left_ref[...] = packed_edge(along[:, :BLK], 0)
    to_right_ref[...] = packed_edge(along[:, CX - BLK:], BLK - 32)


def third_kernel(recv_ref, dose_ref, along_ref, density_ref, from_left_ref, from_right_ref, rtaps_ref, field_ref, final_ref):
    field = field_of(along_ref, from_left_ref, from_right_ref, rtaps_ref)
    field_ref[...] = field
    place, _ = slots(recv_ref, REACH)
    exposure = gathered(density_ref[...] + BACKSCATTER * field, decoded(place), None)
    final_ref[:, 0, :] = corrected(dose_ref[...], exposure)


def unpack_kernel(ret_ref, owner_ref, rank_ref, out_ref):
    mine = owner_ref[...] == lax.broadcasted_iota(jnp.int32, (N_ROW, S_DEV), 0)
    at_rank = jnp.where(rank_ref[...] == lax.broadcasted_iota(jnp.int32, (CAP, S_DEV), 0).astype(F32), 1.0, 0.0).astype(BF)
    parts = jnp.concatenate([p.astype(BF) for p in split3(ret_ref[:, 0, :])], 0)
    g = nn_dot(parts, at_rank)
    whole = g[:N_ROW] + g[N_ROW:2 * N_ROW] + g[2 * N_ROW:]
    out_ref[...] = jnp.sum(jnp.where(mine, whole, 0.0), axis=0, keepdims=True)


def vmem():
    return pl.BlockSpec(memory_space=pltpu.VMEM)


def call(kernel, outs, n_in, scratch=()):
    return pl.pallas_call(
        kernel,
        out_shape=[jax.ShapeDtypeStruct(s, F32) for s in outs],
        in_specs=[vmem()] * n_in,
        out_specs=[vmem() for _ in outs],
        scratch_shapes=list(scratch),
        compiler_params=pltpu.CompilerParams(vmem_limit_bytes=48 << 20),
    )


def exchanged(to_left, to_right):
    n = lax.axis_size("col")
    from_left = lax.ppermute(to_right, "col", [(i, (i + 1) % n) for i in range(n)])
    from_right = lax.ppermute(to_left, "col", [((i + 1) % n, i) for i in range(n)])
    return from_left, from_right


def per_device(shot_dose, shot_owner, shot_cell, shot_offset):
    owner = shot_owner.reshape(1, S_DEV)
    ltaps = jnp.asarray(left_constant(3 * CY, NT * CY, CY))
    ltaps2 = jnp.asarray(left_constant(CY, 3 * CY, CY))
    rtaps = jnp.asarray(right_constant())
    send, rank = call(pack_kernel, [(N_ROW, 1, 2 * NT * CAP), (1, S_DEV)], 4)(
        shot_dose.reshape(1, S_DEV), owner, shot_cell.reshape(1, S_DEV), shot_offset.reshape(1, S_DEV)
    )
    recv = lax.all_to_all(send, "row", split_axis=0, concat_axis=0, tiled=True)
    edge = (3 * CY // 4, BLK)
    along, density, to_left, to_right = call(first_kernel, [(3 * CY, CX), (3 * CY, CX), edge, edge], 2)(recv, ltaps)
    from_left, from_right = exchanged(to_left, to_right)
    edge = (CY // 4, BLK)
    dose, along, density, to_left, to_right = call(
        second_kernel, [(N_ROW, CAP), (CY, CX), (CY, CX), edge, edge], 7, (pltpu.VMEM((XR, SLOTS), BF),)
    )(recv, along, density, from_left, from_right, rtaps, ltaps2)
    from_left, from_right = exchanged(to_left, to_right)
    field, final = call(third_kernel, [(CY, CX), (N_ROW, 1, CAP)], 7)(
        recv, dose, along, density, from_left, from_right, rtaps
    )
    back = lax.all_to_all(final, "row", split_axis=0, concat_axis=0, tiled=True)
    (out,) = call(unpack_kernel, [(1, S_DEV)], 3)(back, owner, rank)
    return out.reshape(S_DEV), field


def solution(mesh):
    placed = (P(("row", "col")), P(("row", "col"), None), P(("row", "col")), P(("row", "col")))
    return jax.shard_map(
        per_device,
        mesh=mesh,
        in_specs=placed,
        out_specs=(P(("row", "col")), P("row", "col")),
        check_vma=False,
    )
```

```python
import jax
import jax.numpy as jnp
import numpy as np
from jax import lax
from jax.experimental import pallas as pl
from jax.experimental.pallas import tpu as pltpu
from jax.sharding import PartitionSpec as P

CY = 32
CX = 512
HALF = 30
N_ROW = 32
N_COL = 8
S_DEV = 2048
CAP = 128
REACH = 2
NT = 2 * REACH + 1
BLK = 128
NB = CX // BLK
XR = BLK + 16
SLOTS = N_ROW * CAP
SUB16 = 16
BF = jnp.bfloat16
F32 = jnp.float32

BACKSCATTER = 0.6
SPREAD = 10.0


def taps():
    lags = np.arange(2 * HALF + 1, dtype=np.float64) - HALF
    values = np.exp(-(lags * lags) / (2.0 * SPREAD * SPREAD))
    return values / values.sum()


def band(rows, cols, offset):
    lag = np.arange(cols)[None, :] - np.arange(rows)[:, None] - offset + HALF
    t = taps()
    return np.where((lag >= 0) & (lag <= 2 * HALF), t[np.clip(lag, 0, 2 * HALF)], 0.0)


def two(m):
    hi = m.astype(jnp.bfloat16)
    lo = (m - hi.astype(np.float64)).astype(jnp.bfloat16)
    return np.asarray(hi), np.asarray(lo)


def left_constant(rows, cols, offset):
    hi, lo = two(band(rows, cols, offset))
    return np.concatenate([np.concatenate([hi, hi], 1), np.concatenate([lo, lo], 1)], 0)


def right_constant():
    hi, lo = two(band(BLK, 3 * BLK, BLK).T)
    return np.concatenate([hi, lo], 1)


def split2(v):
    hi = v.astype(BF)
    lo = (v - hi.astype(F32)).astype(BF)
    return hi, lo


def split3(v):
    hi = v.astype(BF).astype(F32)
    rest = v - hi
    mid = rest.astype(BF).astype(F32)
    return hi, mid, rest - mid


def nt_dot(a, b):
    return lax.dot_general(a, b, (((1,), (1,)), ((), ())), preferred_element_type=F32)


def nn_dot(a, b):
    return lax.dot_general(a, b, (((1,), (0,)), ((), ())), preferred_element_type=F32)


def shifted_rows(v, by):
    if by == 0:
        return v
    pad = jnp.zeros((abs(by), v.shape[1]), v.dtype)
    return jnp.concatenate([v[by:], pad], 0) if by > 0 else jnp.concatenate([pad, v[:by]], 0)


def repeated(row):
    return jnp.broadcast_to(row, (SUB16, row.shape[1])).astype(BF)


def numbers(first, width):
    return (lax.broadcasted_iota(jnp.int32, (SUB16, width), 0) + first).astype(F32).astype(BF)


def equal_rows(row, rows):
    wide = repeated(row)
    return [numbers(SUB16 * k, row.shape[1]) == wide for k in range(rows // SUB16)]


def chosen(masks, row):
    wide = repeated(row)
    none = jnp.zeros_like(wide)
    return jnp.concatenate([jnp.where(m, wide, none) for m in masks], 0)


def pack_kernel(dose_hbm, owner_hbm, cell_hbm, offset_hbm, send_ref, rank_ref, owner_ref,
                dose_v, owner_v, cell_v, offset_v, sems):
    copies = [pltpu.make_async_copy(src, dst, sems.at[n]) for n, (src, dst) in enumerate(
        ((owner_hbm, owner_v), (cell_hbm, cell_v), (offset_hbm, offset_v), (dose_hbm, dose_v)))]
    for copy in copies:
        copy.start()
    chunk = 256
    n_chunks = S_DEV // chunk
    rows_at = lax.broadcasted_iota(jnp.int32, (chunk, chunk), 0)
    cols_at = lax.broadcasted_iota(jnp.int32, (chunk, chunk), 1)
    before = jnp.where(rows_at < cols_at, 1.0, 0.0).astype(BF)
    copies[0].wait()
    owner = owner_v[...].astype(F32)
    owner_ref[...] = owner
    mine = equal_rows(owner, N_ROW)
    ones = chosen(mine, jnp.ones((1, S_DEV), F32))
    stacked = jnp.concatenate([ones[:, c * chunk:(c + 1) * chunk] for c in range(n_chunks)], 0)
    prefix = nn_dot(stacked, before)
    totals = nn_dot(stacked, jnp.ones((chunk, chunk), BF))
    base = jnp.zeros((N_ROW, chunk), F32)
    ranks = []
    for c in range(n_chunks):
        here = slice(c * N_ROW, (c + 1) * N_ROW)
        inside = ones[:, c * chunk:(c + 1) * chunk].astype(F32)
        ranks.append(jnp.sum(inside * (prefix[here] + base), axis=0, keepdims=True))
        base = base + totals[here]
    rank = jnp.concatenate(ranks, 1)
    rank_ref[...] = rank
    at_rank = chosen(equal_rows(rank, CAP), jnp.ones((1, S_DEV), F32))
    for copy in copies[1:]:
        copy.wait()
    place = (cell_v[...] * 256 + offset_v[...]).astype(F32)
    dose = dose_v[...]
    parts = [chosen(mine, part) for part in split3(place) + split3(dose)]
    packed = nt_dot(jnp.concatenate(parts, 0), at_rank)
    for which in range(2):
        p = packed[3 * which * N_ROW:3 * (which + 1) * N_ROW]
        whole = p[:N_ROW] + p[N_ROW:2 * N_ROW] + p[2 * N_ROW:]
        for t in range(NT):
            start = (2 * t + which) * CAP
            send_ref[:, 0, start:start + CAP] = shifted_rows(whole, t - REACH)


def decoded(place):
    cell = jnp.floor(place * (1.0 / 256.0))
    fine = place - 256.0 * cell
    cell_y = jnp.floor((cell + 0.5) * (1.0 / (CX - 1)))
    cell_x = cell - (CX - 1) * cell_y
    off_y = jnp.floor(fine * (1.0 / 16.0))
    off_x = fine - 16.0 * off_y
    block = jnp.floor(cell_x * (1.0 / BLK))
    column = cell_x - BLK * block
    off_y, off_x = off_y * (1.0 / 16.0), off_x * (1.0 / 16.0)
    return dict(block=block, y=cell_y, y1=cell_y + 1.0, column=column, column1=column + 1.0,
                y0w=1.0 - off_y, y1w=off_y, x0=1.0 - off_x, x1=off_x)


def pair_columns(shot):
    return lambda i: jnp.concatenate([column_chunk(shot, i), column_chunk(shot, i + 1)], 1)


def over_rows(v, i):
    return jnp.broadcast_to(v[i:i + 1], (SUB16, CAP)).astype(BF)


def row_numbers(first):
    return (lax.broadcasted_iota(jnp.int32, (SUB16, CAP), 0) + first).astype(F32).astype(BF)


def column_chunk(shot, i):
    first, second = over_rows(shot["column"], i), over_rows(shot["column1"], i)
    w0, w1 = over_rows(shot["x0"], i), over_rows(shot["x1"], i)
    none = jnp.zeros_like(w0)
    out = []
    for k in range(XR // SUB16):
        at = row_numbers(SUB16 * k)
        out.append(jnp.where(at == first, w0, jnp.where(at == second, w1, none)))
    return jnp.concatenate(out, 0)


def row_chunk(shot, dosed, i):
    first, second = over_rows(shot["y"], i), over_rows(shot["y1"], i)
    block = over_rows(shot["block"], i)
    values = [over_rows(v, i) for v in dosed]
    none = jnp.zeros_like(first)
    parts = [[], []]
    for k in range(CY // SUB16):
        at = row_numbers(SUB16 * k)
        on_first, on_second = at == first, at == second
        for part in range(2):
            q0, q1 = values[2 * part:2 * part + 2]
            parts[part].append(jnp.where(on_first, q0, jnp.where(on_second, q1, none)))
    inside = [block == jnp.full((SUB16, CAP), h, F32).astype(BF) for h in range(NB)]
    return jnp.concatenate([jnp.where(inside[h], v, none) for part in parts for h in range(NB) for v in part], 0)


def dosed_weights(shot, dose):
    hi0, lo0 = split2(shot["y0w"] * dose)
    hi1, lo1 = split2(shot["y1w"] * dose)
    return [v.astype(F32) for v in (hi0, hi1, lo0, lo1)]


def tile_density(shot, dose, columns):
    dosed = dosed_weights(shot, dose)
    both = None
    for i in range(0, N_ROW, 2):
        a = jnp.concatenate([row_chunk(shot, dosed, i), row_chunk(shot, dosed, i + 1)], 1)
        one = nt_dot(a, columns(i))
        both = one if both is None else both + one
    d = both[:BLK] + both[BLK:]
    blocks = [d[:CY, :BLK]]
    for h in range(1, NB):
        over = d[(h - 1) * CY:h * CY, BLK:XR]
        over = jnp.concatenate([over, jnp.zeros((CY, BLK - XR + BLK), F32)], 1)
        blocks.append(d[h * CY:(h + 1) * CY, :BLK] + over)
    return jnp.concatenate(blocks, 1)


def packed_edge(block, lane0):
    rows = block.shape[0] // 4
    lane = lax.broadcasted_iota(jnp.int32, (rows, BLK), 1)
    out = jnp.zeros((rows, BLK), block.dtype)
    for g in range(4):
        part = block[g * rows:(g + 1) * rows]
        shift = (32 * g - lane0) % BLK
        part = pltpu.roll(part, shift, 1) if shift else part
        out = jnp.where(lane // 32 == g, part, out)
    return out


def unpacked_edge(edge, lane0):
    parts = []
    for g in range(4):
        shift = (lane0 - 32 * g) % BLK
        parts.append(pltpu.roll(edge, shift, 1) if shift else edge)
    return jnp.concatenate(parts, 0)


def blurred_y(density, taps_ref):
    hi, lo = split2(density)
    both = nn_dot(taps_ref[...], jnp.concatenate([hi, lo], 0))
    rows = both.shape[0] // 2
    return both[:rows] + both[rows:]


def blurred_x(along_y, left, right, taps_ref):
    wide = jnp.concatenate([left, along_y, right], 1)
    rows = along_y.shape[0]
    stacked = jnp.concatenate([wide[:, h * BLK:(h + 3) * BLK] for h in range(NB)], 0)
    hi, lo = split2(stacked)
    both = nn_dot(jnp.concatenate([hi, lo], 0), taps_ref[...])
    both = both[:NB * rows] + both[NB * rows:]
    out = both[:, :BLK] + both[:, BLK:]
    return jnp.concatenate([out[h * rows:(h + 1) * rows] for h in range(NB)], 1)


def gathered(total, shot, b_ref):
    pieces = []
    for h in range(NB):
        inside = total[:, h * BLK:(h + 1) * BLK]
        if h + 1 < NB:
            after = total[:, (h + 1) * BLK:(h + 1) * BLK + XR - BLK]
        else:
            after = jnp.zeros((CY, XR - BLK), F32)
        pieces.append(jnp.concatenate([inside, after], 1))
    hi, lo = split2(jnp.concatenate(pieces, 0))
    table = jnp.concatenate([hi, lo], 0)
    at = lax.broadcasted_iota(jnp.int32, (CY, CAP), 0).astype(F32)
    rows = []
    for i in range(0, N_ROW, 2):
        columns = pair_columns(shot)(i)
        if b_ref is not None:
            b_ref[:, i * CAP:(i + 2) * CAP] = columns
        both = nn_dot(table, columns)
        for j in range(2):
            here = slice(j * CAP, (j + 1) * CAP)
            g = both[:BLK, here] + both[BLK:, here]
            block = shot["block"][i + j:i + j + 1]
            mine = g[:CY]
            for h in range(1, NB):
                mine = jnp.where(block == float(h), g[h * CY:(h + 1) * CY], mine)
            y, y1 = shot["y"][i + j:i + j + 1], shot["y1"][i + j:i + j + 1]
            w = jnp.where(at == y, shot["y0w"][i + j:i + j + 1], jnp.where(at == y1, shot["y1w"][i + j:i + j + 1], 0.0))
            rows.append(jnp.sum(w * mine, axis=0, keepdims=True))
    return jnp.concatenate(rows, 0)


def corrected(dose, exposure):
    return jnp.where(dose > 0.0, dose * (1.0 + BACKSCATTER) / exposure, 0.0)


def slots(recv_ref, t):
    start = 2 * t * CAP
    return recv_ref[:, 0, start:start + CAP], recv_ref[:, 0, start + CAP:start + 2 * CAP]


def first_kernel(recv_ref, ltaps_ref, along_ref, density_ref, to_left_ref, to_right_ref):
    tiles = []
    for t in range(NT):
        place, dose = slots(recv_ref, t)
        shot = decoded(place)
        tiles.append(tile_density(shot, dose, pair_columns(shot)))
    density_ref[...] = jnp.concatenate(tiles[1:NT - 1], 0)
    along = blurred_y(jnp.concatenate(tiles, 0), ltaps_ref)
    along_ref[...] = along
    to_left_ref[...] = packed_edge(along[:, :BLK], 0)
    to_right_ref[...] = packed_edge(along[:, CX - BLK:], BLK - 32)


def field_of(along_ref, from_left_ref, from_right_ref, rtaps_ref):
    col = lax.axis_index("col")
    left = unpacked_edge(jnp.where(col > 0, from_left_ref[...], 0.0), BLK - 32)
    right = unpacked_edge(jnp.where(col < N_COL - 1, from_right_ref[...], 0.0), 0)
    return blurred_x(along_ref[...], left, right, rtaps_ref)


def second_kernel(recv_ref, along_ref, density_ref, from_left_ref, from_right_ref, rtaps_ref, ltaps_ref,
                  dose_ref, along2_ref, density2_ref, to_left_ref, to_right_ref, b_ref):
    total = density_ref[...] + BACKSCATTER * field_of(along_ref, from_left_ref, from_right_ref, rtaps_ref)
    tiles = []
    for n in range(NT - 2):
        place, dose = slots(recv_ref, n + 1)
        shot = decoded(place)
        exposure = gathered(total[n * CY:(n + 1) * CY], shot, b_ref)
        dose = corrected(dose, exposure)
        if n + 1 == REACH:
            dose_ref[...] = dose
        tiles.append(tile_density(shot, dose, lambda i: b_ref[:, i * CAP:(i + 2) * CAP]))
    density2_ref[...] = tiles[1]
    along = blurred_y(jnp.concatenate(tiles, 0), ltaps_ref)
    along2_ref[...] = along
    to_left_ref[...] = packed_edge(along[:, :BLK], 0)
    to_right_ref[...] = packed_edge(along[:, CX - BLK:], BLK - 32)


def third_kernel(recv_ref, dose_ref, along_ref, density_ref, from_left_ref, from_right_ref, rtaps_ref, field_ref, final_ref):
    field = field_of(along_ref, from_left_ref, from_right_ref, rtaps_ref)
    field_ref[...] = field
    place, _ = slots(recv_ref, REACH)
    exposure = gathered(density_ref[...] + BACKSCATTER * field, decoded(place), None)
    final_ref[:, 0, :] = corrected(dose_ref[...], exposure)


def unpack_kernel(ret_ref, owner_ref, rank_ref, out_ref):
    at_rank = chosen(equal_rows(rank_ref[...], CAP), jnp.ones((1, S_DEV), F32))
    parts = jnp.concatenate([p.astype(BF) for p in split3(ret_ref[:, 0, :])], 0)
    g = nn_dot(parts, at_rank)
    whole = g[:N_ROW] + g[N_ROW:2 * N_ROW] + g[2 * N_ROW:]
    mine = owner_ref[...] == lax.broadcasted_iota(jnp.int32, (N_ROW, S_DEV), 0).astype(F32)
    out_ref[...] = jnp.sum(jnp.where(mine, whole, 0.0), axis=0, keepdims=True)


def vmem():
    return pl.BlockSpec(memory_space=pltpu.VMEM)


def call(kernel, outs, n_in, scratch=(), space=pltpu.VMEM):
    return pl.pallas_call(
        kernel,
        out_shape=[jax.ShapeDtypeStruct(s, F32) for s in outs],
        in_specs=[pl.BlockSpec(memory_space=space)] * n_in,
        out_specs=[vmem() for _ in outs],
        scratch_shapes=list(scratch),
        compiler_params=pltpu.CompilerParams(vmem_limit_bytes=48 << 20),
    )


def exchanged(to_left, to_right):
    n = lax.axis_size("col")
    from_left = lax.ppermute(to_right, "col", [(i, (i + 1) % n) for i in range(n)])
    from_right = lax.ppermute(to_left, "col", [((i + 1) % n, i) for i in range(n)])
    return from_left, from_right


def per_device(shot_dose, shot_owner, shot_cell, shot_offset):
    ltaps = jnp.asarray(left_constant(3 * CY, NT * CY, CY))
    ltaps2 = jnp.asarray(left_constant(CY, 3 * CY, CY))
    rtaps = jnp.asarray(right_constant())
    row = (1, S_DEV)
    rows = [pltpu.VMEM(row, F32)] + [pltpu.VMEM(row, jnp.int32)] * 3 + [pltpu.SemaphoreType.DMA((4,))]
    send, rank, owner = call(pack_kernel, [(N_ROW, 1, 2 * NT * CAP), row, row], 4, rows, pltpu.HBM)(
        *(pltpu.with_memory_space_constraint(v.reshape(row), pltpu.HBM) for v in (shot_dose, shot_owner, shot_cell, shot_offset))
    )
    recv = lax.all_to_all(send, "row", split_axis=0, concat_axis=0, tiled=True)
    edge = (3 * CY // 4, BLK)
    along, density, to_left, to_right = call(first_kernel, [(3 * CY, CX), (3 * CY, CX), edge, edge], 2)(recv, ltaps)
    from_left, from_right = exchanged(to_left, to_right)
    edge = (CY // 4, BLK)
    dose, along, density, to_left, to_right = call(
        second_kernel, [(N_ROW, CAP), (CY, CX), (CY, CX), edge, edge], 7, (pltpu.VMEM((XR, SLOTS), BF),)
    )(recv, along, density, from_left, from_right, rtaps, ltaps2)
    from_left, from_right = exchanged(to_left, to_right)
    field, final = call(third_kernel, [(CY, CX), (N_ROW, 1, CAP)], 7)(
        recv, dose, along, density, from_left, from_right, rtaps
    )
    back = lax.all_to_all(final, "row", split_axis=0, concat_axis=0, tiled=True)
    (out,) = call(unpack_kernel, [(1, S_DEV)], 3)(back, owner, rank)
    return out.reshape(S_DEV), field


def solution(mesh):
    placed = (P(("row", "col")), P(("row", "col"), None), P(("row", "col")), P(("row", "col")))
    return jax.shard_map(
        per_device,
        mesh=mesh,
        in_specs=placed,
        out_specs=(P(("row", "col")), P("row", "col")),
        check_vma=False,
    )
```

```python
import jax
import jax.numpy as jnp
import numpy as np
from jax import lax
from jax.experimental import pallas as pl
from jax.experimental.pallas import tpu as pltpu
from jax.sharding import PartitionSpec as P

CY = 32
CX = 512
HALF = 30
N_ROW = 32
N_COL = 8
S_DEV = 2048
CAP = 128
REACH = 2
NT = 2 * REACH + 1
BLK = 128
NB = CX // BLK
XR = BLK + 16
SLOTS = N_ROW * CAP
GROUP = 8
SUB16 = 16
BF = jnp.bfloat16
F32 = jnp.float32

BACKSCATTER = 0.6
SPREAD = 10.0


def taps():
    lags = np.arange(2 * HALF + 1, dtype=np.float64) - HALF
    values = np.exp(-(lags * lags) / (2.0 * SPREAD * SPREAD))
    return values / values.sum()


def band(rows, cols, offset):
    lag = np.arange(cols)[None, :] - np.arange(rows)[:, None] - offset + HALF
    t = taps()
    return np.where((lag >= 0) & (lag <= 2 * HALF), t[np.clip(lag, 0, 2 * HALF)], 0.0)


def two(m):
    hi = m.astype(jnp.bfloat16)
    lo = (m - hi.astype(np.float64)).astype(jnp.bfloat16)
    return np.asarray(hi), np.asarray(lo)


def left_constant(rows, cols, offset):
    hi, lo = two(band(rows, cols, offset))
    return np.concatenate([np.concatenate([hi, hi], 1), np.concatenate([lo, lo], 1)], 0)


def right_constant():
    hi, lo = two(band(BLK, 3 * BLK, BLK).T)
    return np.concatenate([hi, lo], 1)


def split2(v):
    hi = v.astype(BF)
    lo = (v - hi.astype(F32)).astype(BF)
    return hi, lo


def split3(v):
    hi = v.astype(BF).astype(F32)
    rest = v - hi
    mid = rest.astype(BF).astype(F32)
    return hi, mid, rest - mid


def nt_dot(a, b):
    return lax.dot_general(a, b, (((1,), (1,)), ((), ())), preferred_element_type=F32)


def nn_dot(a, b):
    return lax.dot_general(a, b, (((1,), (0,)), ((), ())), preferred_element_type=F32)


def shifted_rows(v, by):
    if by == 0:
        return v
    pad = jnp.zeros((abs(by), v.shape[1]), v.dtype)
    return jnp.concatenate([v[by:], pad], 0) if by > 0 else jnp.concatenate([pad, v[:by]], 0)


def repeated(row):
    return jnp.broadcast_to(row, (SUB16, row.shape[1])).astype(BF)


def numbers(first, width):
    return (lax.broadcasted_iota(jnp.int32, (SUB16, width), 0) + first).astype(F32).astype(BF)


def equal_rows(row, rows):
    wide = repeated(row)
    return [numbers(SUB16 * k, row.shape[1]) == wide for k in range(rows // SUB16)]


def chosen(masks, row):
    wide = repeated(row)
    none = jnp.zeros_like(wide)
    return jnp.concatenate([jnp.where(m, wide, none) for m in masks], 0)


def pack_kernel(dose_hbm, owner_hbm, cell_hbm, offset_hbm, send_ref, rank_ref, owner_ref,
                dose_v, owner_v, cell_v, offset_v, sems):
    copies = [pltpu.make_async_copy(src, dst, sems.at[n]) for n, (src, dst) in enumerate(
        ((owner_hbm, owner_v), (cell_hbm, cell_v), (offset_hbm, offset_v), (dose_hbm, dose_v)))]
    for copy in copies:
        copy.start()
    chunk = 256
    n_chunks = S_DEV // chunk
    rows_at = lax.broadcasted_iota(jnp.int32, (chunk, chunk), 0)
    cols_at = lax.broadcasted_iota(jnp.int32, (chunk, chunk), 1)
    before = jnp.where(rows_at < cols_at, 1.0, 0.0).astype(BF)
    copies[0].wait()
    owner = owner_v[...].astype(F32)
    owner_ref[...] = owner
    mine = equal_rows(owner, N_ROW)
    ones = chosen(mine, jnp.ones((1, S_DEV), F32))
    stacked = jnp.concatenate([ones[:, c * chunk:(c + 1) * chunk] for c in range(n_chunks)], 0)
    prefix = nn_dot(stacked, before)
    totals = nn_dot(stacked, jnp.ones((chunk, chunk), BF))
    base = jnp.zeros((N_ROW, chunk), F32)
    ranks = []
    for c in range(n_chunks):
        here = slice(c * N_ROW, (c + 1) * N_ROW)
        inside = ones[:, c * chunk:(c + 1) * chunk].astype(F32)
        ranks.append(jnp.sum(inside * (prefix[here] + base), axis=0, keepdims=True))
        base = base + totals[here]
    rank = jnp.concatenate(ranks, 1)
    rank_ref[...] = rank
    at_rank = chosen(equal_rows(rank, CAP), jnp.ones((1, S_DEV), F32))
    for copy in copies[1:]:
        copy.wait()
    place = (cell_v[...] * 256 + offset_v[...]).astype(F32)
    dose = dose_v[...]
    parts = [chosen(mine, part) for part in split3(place) + split3(dose)]
    packed = nt_dot(jnp.concatenate(parts, 0), at_rank)
    for which in range(2):
        p = packed[3 * which * N_ROW:3 * (which + 1) * N_ROW]
        whole = p[:N_ROW] + p[N_ROW:2 * N_ROW] + p[2 * N_ROW:]
        for t in range(NT):
            start = (2 * t + which) * CAP
            send_ref[:, 0, start:start + CAP] = shifted_rows(whole, t - REACH)


def decoded(place):
    cell = jnp.floor(place * (1.0 / 256.0))
    fine = place - 256.0 * cell
    cell_y = jnp.floor((cell + 0.5) * (1.0 / (CX - 1)))
    cell_x = cell - (CX - 1) * cell_y
    off_y = jnp.floor(fine * (1.0 / 16.0))
    off_x = fine - 16.0 * off_y
    block = jnp.floor(cell_x * (1.0 / BLK))
    column = cell_x - BLK * block
    off_y, off_x = off_y * (1.0 / 16.0), off_x * (1.0 / 16.0)
    return dict(block=block, y=cell_y, y1=cell_y + 1.0, column=column, column1=column + 1.0,
                y0w=1.0 - off_y, y1w=off_y, x0=1.0 - off_x, x1=off_x)


def pair_columns(shot, i):
    return jnp.concatenate([column_chunk(shot, i), column_chunk(shot, i + 1)], 1)


def over_rows(v, i):
    return jnp.broadcast_to(v[i:i + 1], (SUB16, CAP)).astype(BF)


def row_numbers(first):
    return (lax.broadcasted_iota(jnp.int32, (SUB16, CAP), 0) + first).astype(F32).astype(BF)


def column_chunk(shot, i):
    first, second = over_rows(shot["column"], i), over_rows(shot["column1"], i)
    w0, w1 = over_rows(shot["x0"], i), over_rows(shot["x1"], i)
    none = jnp.zeros_like(w0)
    out = []
    for k in range(XR // SUB16):
        at = row_numbers(SUB16 * k)
        out.append(jnp.where(at == first, w0, jnp.where(at == second, w1, none)))
    return jnp.concatenate(out, 0)


def row_chunk(shot, dosed, i, at_dosed):
    first, second = over_rows(shot["y"], i), over_rows(shot["y1"], i)
    block = over_rows(shot["block"], i)
    values = [over_rows(v, at_dosed) for v in dosed]
    none = jnp.zeros_like(first)
    parts = [[], []]
    for k in range(CY // SUB16):
        at = row_numbers(SUB16 * k)
        on_first, on_second = at == first, at == second
        for part in range(2):
            q0, q1 = values[2 * part:2 * part + 2]
            parts[part].append(jnp.where(on_first, q0, jnp.where(on_second, q1, none)))
    inside = [block == jnp.full((SUB16, CAP), h, F32).astype(BF) for h in range(NB)]
    return jnp.concatenate([jnp.where(inside[h], v, none) for part in parts for h in range(NB) for v in part], 0)


def dosed_weights(shot, dose, sources=slice(None)):
    hi0, lo0 = split2(shot["y0w"][sources] * dose)
    hi1, lo1 = split2(shot["y1w"][sources] * dose)
    return [v.astype(F32) for v in (hi0, hi1, lo0, lo1)]


def density_pair(shot, dosed, first, i, columns):
    a = jnp.concatenate([row_chunk(shot, dosed, j, j - first) for j in (i, i + 1)], 1)
    return nt_dot(a, columns)


def assembled(both):
    d = both[:BLK] + both[BLK:]
    blocks = [d[:CY, :BLK]]
    for h in range(1, NB):
        over = d[(h - 1) * CY:h * CY, BLK:XR]
        over = jnp.concatenate([over, jnp.zeros((CY, BLK - XR + BLK), F32)], 1)
        blocks.append(d[h * CY:(h + 1) * CY, :BLK] + over)
    return jnp.concatenate(blocks, 1)


def added(total, one):
    return one if total is None else total + one


def tile_density(shot, dose):
    dosed = dosed_weights(shot, dose)
    both = None
    for i in range(0, N_ROW, 2):
        both = added(both, density_pair(shot, dosed, 0, i, pair_columns(shot, i)))
    return assembled(both)


def packed_edge(block, lane0):
    rows = block.shape[0] // 4
    lane = lax.broadcasted_iota(jnp.int32, (rows, BLK), 1)
    out = jnp.zeros((rows, BLK), block.dtype)
    for g in range(4):
        part = block[g * rows:(g + 1) * rows]
        shift = (32 * g - lane0) % BLK
        part = pltpu.roll(part, shift, 1) if shift else part
        out = jnp.where(lane // 32 == g, part, out)
    return out


def unpacked_edge(edge, lane0):
    parts = []
    for g in range(4):
        shift = (lane0 - 32 * g) % BLK
        parts.append(pltpu.roll(edge, shift, 1) if shift else edge)
    return jnp.concatenate(parts, 0)


def blurred_y(density, taps_ref):
    hi, lo = split2(density)
    both = nn_dot(taps_ref[...], jnp.concatenate([hi, lo], 0))
    rows = both.shape[0] // 2
    return both[:rows] + both[rows:]


def blurred_x(along_y, left, right, taps_ref):
    wide = jnp.concatenate([left, along_y, right], 1)
    rows = along_y.shape[0]
    stacked = jnp.concatenate([wide[:, h * BLK:(h + 3) * BLK] for h in range(NB)], 0)
    hi, lo = split2(stacked)
    both = nn_dot(jnp.concatenate([hi, lo], 0), taps_ref[...])
    both = both[:NB * rows] + both[NB * rows:]
    out = both[:, :BLK] + both[:, BLK:]
    return jnp.concatenate([out[h * rows:(h + 1) * rows] for h in range(NB)], 1)


def gather_table(total):
    pieces = []
    for h in range(NB):
        inside = total[:, h * BLK:(h + 1) * BLK]
        if h + 1 < NB:
            after = total[:, (h + 1) * BLK:(h + 1) * BLK + XR - BLK]
        else:
            after = jnp.zeros((CY, XR - BLK), F32)
        pieces.append(jnp.concatenate([inside, after], 1))
    return jnp.concatenate(split2(jnp.concatenate(pieces, 0)), 0)


def gather_pair(table, shot, i, columns):
    both = nn_dot(table, columns)
    at = lax.broadcasted_iota(jnp.int32, (CY, CAP), 0).astype(F32)
    rows = []
    for j in range(2):
        here = slice(j * CAP, (j + 1) * CAP)
        g = both[:BLK, here] + both[BLK:, here]
        block, y, y1, w0, w1 = (shot[name][i + j:i + j + 1] for name in ("block", "y", "y1", "y0w", "y1w"))
        mine = g[:CY]
        for h in range(1, NB):
            mine = jnp.where(block == float(h), g[h * CY:(h + 1) * CY], mine)
        w = jnp.where(at == y, w0, jnp.where(at == y1, w1, 0.0))
        rows.append(jnp.sum(w * mine, axis=0, keepdims=True))
    return rows


def corrected(dose, exposure):
    return jnp.where(dose > 0.0, dose * (1.0 + BACKSCATTER) / exposure, 0.0)


def slots(recv_ref, t):
    start = 2 * t * CAP
    return recv_ref[:, 0, start:start + CAP], recv_ref[:, 0, start + CAP:start + 2 * CAP]


def first_kernel(recv_ref, ltaps_ref, along_ref, density_ref, to_left_ref, to_right_ref):
    tiles = []
    for t in range(NT):
        place, dose = slots(recv_ref, t)
        shot = decoded(place)
        tiles.append(tile_density(shot, dose))
    density_ref[...] = jnp.concatenate(tiles[1:NT - 1], 0)
    along = blurred_y(jnp.concatenate(tiles, 0), ltaps_ref)
    along_ref[...] = along
    to_left_ref[...] = packed_edge(along[:, :BLK], 0)
    to_right_ref[...] = packed_edge(along[:, CX - BLK:], BLK - 32)


def field_of(along_ref, from_left_ref, from_right_ref, rtaps_ref):
    col = lax.axis_index("col")
    left = unpacked_edge(jnp.where(col > 0, from_left_ref[...], 0.0), BLK - 32)
    right = unpacked_edge(jnp.where(col < N_COL - 1, from_right_ref[...], 0.0), 0)
    return blurred_x(along_ref[...], left, right, rtaps_ref)


def second_kernel(recv_ref, along_ref, density_ref, from_left_ref, from_right_ref, rtaps_ref, ltaps_ref,
                  dose_ref, along2_ref, density2_ref, to_left_ref, to_right_ref, b_ref):
    total = density_ref[...] + BACKSCATTER * field_of(along_ref, from_left_ref, from_right_ref, rtaps_ref)
    places = [slots(recv_ref, n + 1) for n in range(NT - 2)]
    shots = [decoded(place) for place, _ in places]
    tables = [gather_table(total[n * CY:(n + 1) * CY]) for n in range(NT - 2)]
    densities = [None] * (NT - 2)
    groups = [(n, first) for n in range(NT - 2) for first in range(0, N_ROW, GROUP)]
    dosed = None
    for step in range(len(groups) + 1):
        rows = []
        for j in range(0, GROUP, 2):
            if step < len(groups):
                n, first = groups[step]
                columns = pair_columns(shots[n], first + j)
                b_ref[n, :, (first + j) * CAP:(first + j + 2) * CAP] = columns
                rows += gather_pair(tables[n], shots[n], first + j, columns)
            if step > 0:
                m, start = groups[step - 1]
                columns = b_ref[m, :, (start + j) * CAP:(start + j + 2) * CAP]
                densities[m] = added(densities[m], density_pair(shots[m], dosed, start, start + j, columns))
        if rows:
            sources = slice(first, first + GROUP)
            dose = corrected(places[n][1][sources], jnp.concatenate(rows, 0))
            if n + 1 == REACH:
                dose_ref[sources, :] = dose
            dosed = dosed_weights(shots[n], dose, sources)
    tiles = [assembled(both) for both in densities]
    density2_ref[...] = tiles[1]
    along = blurred_y(jnp.concatenate(tiles, 0), ltaps_ref)
    along2_ref[...] = along
    to_left_ref[...] = packed_edge(along[:, :BLK], 0)
    to_right_ref[...] = packed_edge(along[:, CX - BLK:], BLK - 32)


def third_kernel(recv_ref, dose_ref, along_ref, density_ref, from_left_ref, from_right_ref, rtaps_ref, field_hbm, final_ref,
                 field_ref, sem):
    field = field_of(along_ref, from_left_ref, from_right_ref, rtaps_ref)
    field_ref[...] = field
    copy = pltpu.make_async_copy(field_ref, field_hbm, sem)
    copy.start()
    shot = decoded(slots(recv_ref, REACH)[0])
    table = gather_table(density_ref[...] + BACKSCATTER * field)
    rows = []
    for i in range(0, N_ROW, 2):
        rows += gather_pair(table, shot, i, pair_columns(shot, i))
    final_ref[:, 0, :] = corrected(dose_ref[...], jnp.concatenate(rows, 0))
    copy.wait()


def unpack_kernel(ret_ref, owner_ref, rank_ref, out_ref):
    at_rank = chosen(equal_rows(rank_ref[...], CAP), jnp.ones((1, S_DEV), F32))
    parts = jnp.concatenate([p.astype(BF) for p in split3(ret_ref[:, 0, :])], 0)
    g = nn_dot(parts, at_rank)
    whole = g[:N_ROW] + g[N_ROW:2 * N_ROW] + g[2 * N_ROW:]
    mine = owner_ref[...] == lax.broadcasted_iota(jnp.int32, (N_ROW, S_DEV), 0).astype(F32)
    out_ref[...] = jnp.sum(jnp.where(mine, whole, 0.0), axis=0, keepdims=True)


def call(kernel, outs, n_in, scratch=(), space=pltpu.VMEM, out_spaces=None):
    return pl.pallas_call(
        kernel,
        out_shape=[jax.ShapeDtypeStruct(s, F32) for s in outs],
        in_specs=[pl.BlockSpec(memory_space=space)] * n_in,
        out_specs=[pl.BlockSpec(memory_space=s) for s in out_spaces or [pltpu.VMEM] * len(outs)],
        scratch_shapes=list(scratch),
        compiler_params=pltpu.CompilerParams(vmem_limit_bytes=48 << 20),
    )


def exchanged(to_left, to_right):
    n = lax.axis_size("col")
    from_left = lax.ppermute(to_right, "col", [(i, (i + 1) % n) for i in range(n)])
    from_right = lax.ppermute(to_left, "col", [((i + 1) % n, i) for i in range(n)])
    return from_left, from_right


def per_device(shot_dose, shot_owner, shot_cell, shot_offset):
    ltaps = jnp.asarray(left_constant(3 * CY, NT * CY, CY))
    ltaps2 = jnp.asarray(left_constant(CY, 3 * CY, CY))
    rtaps = jnp.asarray(right_constant())
    row = (1, S_DEV)
    rows = [pltpu.VMEM(row, F32)] + [pltpu.VMEM(row, jnp.int32)] * 3 + [pltpu.SemaphoreType.DMA((4,))]
    send, rank, owner = call(pack_kernel, [(N_ROW, 1, 2 * NT * CAP), row, row], 4, rows, pltpu.HBM)(
        *(pltpu.with_memory_space_constraint(v.reshape(row), pltpu.HBM) for v in (shot_dose, shot_owner, shot_cell, shot_offset))
    )
    recv = lax.all_to_all(send, "row", split_axis=0, concat_axis=0, tiled=True)
    edge = (3 * CY // 4, BLK)
    along, density, to_left, to_right = call(first_kernel, [(3 * CY, CX), (3 * CY, CX), edge, edge], 2)(recv, ltaps)
    from_left, from_right = exchanged(to_left, to_right)
    edge = (CY // 4, BLK)
    dose, along, density, to_left, to_right = call(
        second_kernel, [(N_ROW, CAP), (CY, CX), (CY, CX), edge, edge], 7, (pltpu.VMEM((NT - 2, XR, SLOTS), BF),)
    )(recv, along, density, from_left, from_right, rtaps, ltaps2)
    from_left, from_right = exchanged(to_left, to_right)
    field, final = call(
        third_kernel, [(CY, CX), (N_ROW, 1, CAP)], 7, (pltpu.VMEM((CY, CX), F32), pltpu.SemaphoreType.DMA),
        out_spaces=[pltpu.HBM, pltpu.VMEM],
    )(
        recv, dose, along, density, from_left, from_right, rtaps
    )
    back = lax.all_to_all(final, "row", split_axis=0, concat_axis=0, tiled=True)
    (out,) = call(unpack_kernel, [(1, S_DEV)], 3)(back, owner, rank)
    return out.reshape(S_DEV), field


def solution(mesh):
    placed = (P(("row", "col")), P(("row", "col"), None), P(("row", "col")), P(("row", "col")))
    return jax.shard_map(
        per_device,
        mesh=mesh,
        in_specs=placed,
        out_specs=(P(("row", "col")), P("row", "col")),
        check_vma=False,
    )
```

```python
import jax
import jax.numpy as jnp
import numpy as np
from jax import lax
from jax.experimental import pallas as pl
from jax.experimental.pallas import tpu as pltpu
from jax.sharding import PartitionSpec as P

CY = 32
CX = 512
HALF = 30
N_ROW = 32
N_COL = 8
S_DEV = 2048
CAP = 128
REACH = 2
NT = 2 * REACH + 1
BLK = 128
NB = CX // BLK
XR = BLK + 16
SLOTS = N_ROW * CAP
GROUP = 8
SUB16 = 16
BF = jnp.bfloat16
F32 = jnp.float32

BACKSCATTER = 0.6
SPREAD = 10.0


def taps():
    lags = np.arange(2 * HALF + 1, dtype=np.float64) - HALF
    values = np.exp(-(lags * lags) / (2.0 * SPREAD * SPREAD))
    return values / values.sum()


def band(rows, cols, offset):
    lag = np.arange(cols)[None, :] - np.arange(rows)[:, None] - offset + HALF
    t = taps()
    return np.where((lag >= 0) & (lag <= 2 * HALF), t[np.clip(lag, 0, 2 * HALF)], 0.0)


def two(m):
    hi = m.astype(jnp.bfloat16)
    lo = (m - hi.astype(np.float64)).astype(jnp.bfloat16)
    return np.asarray(hi), np.asarray(lo)


def left_constant(rows, cols, offset):
    hi, lo = two(band(rows, cols, offset))
    return np.concatenate([np.concatenate([hi, hi], 1), np.concatenate([lo, lo], 1)], 0)


def right_constant():
    hi, lo = two(band(BLK, 3 * BLK, BLK).T)
    return np.concatenate([hi, lo], 1)


def split2(v):
    hi = v.astype(BF)
    lo = (v - hi.astype(F32)).astype(BF)
    return hi, lo


def split3(v):
    hi = v.astype(BF).astype(F32)
    rest = v - hi
    mid = rest.astype(BF).astype(F32)
    return hi, mid, rest - mid


def nt_dot(a, b):
    return lax.dot_general(a, b, (((1,), (1,)), ((), ())), preferred_element_type=F32)


def nn_dot(a, b):
    return lax.dot_general(a, b, (((1,), (0,)), ((), ())), preferred_element_type=F32)


def shifted_rows(v, by):
    if by == 0:
        return v
    pad = jnp.zeros((abs(by), v.shape[1]), v.dtype)
    return jnp.concatenate([v[by:], pad], 0) if by > 0 else jnp.concatenate([pad, v[:by]], 0)


def repeated(row):
    return jnp.broadcast_to(row, (SUB16, row.shape[1])).astype(BF)


def numbers(first, width):
    return (lax.broadcasted_iota(jnp.int32, (SUB16, width), 0) + first).astype(F32).astype(BF)


def equal_rows(row, rows):
    wide = repeated(row)
    return [numbers(SUB16 * k, row.shape[1]) == wide for k in range(rows // SUB16)]


def chosen(masks, row):
    wide = repeated(row)
    none = jnp.zeros_like(wide)
    return jnp.concatenate([jnp.where(m, wide, none) for m in masks], 0)


def pack_kernel(dose_hbm, owner_hbm, cell_hbm, offset_hbm, send_ref, rank_ref, owner_ref,
                dose_v, owner_v, cell_v, offset_v, sems):
    copies = [pltpu.make_async_copy(src, dst, sems.at[n]) for n, (src, dst) in enumerate(
        ((owner_hbm, owner_v), (cell_hbm, cell_v), (offset_hbm, offset_v), (dose_hbm, dose_v)))]
    for copy in copies:
        copy.start()
    chunk = 256
    n_chunks = S_DEV // chunk
    rows_at = lax.broadcasted_iota(jnp.int32, (chunk, chunk), 0)
    cols_at = lax.broadcasted_iota(jnp.int32, (chunk, chunk), 1)
    before = jnp.where(rows_at < cols_at, 1.0, 0.0).astype(BF)
    copies[0].wait()
    owner = owner_v[...].astype(F32)
    owner_ref[...] = owner
    mine = equal_rows(owner, N_ROW)
    ones = chosen(mine, jnp.ones((1, S_DEV), F32))
    stacked = jnp.concatenate([ones[:, c * chunk:(c + 1) * chunk] for c in range(n_chunks)], 0)
    prefix = nn_dot(stacked, before)
    totals = nn_dot(stacked, jnp.ones((chunk, chunk), BF))
    base = jnp.zeros((N_ROW, chunk), F32)
    ranks = []
    for c in range(n_chunks):
        here = slice(c * N_ROW, (c + 1) * N_ROW)
        inside = ones[:, c * chunk:(c + 1) * chunk].astype(F32)
        ranks.append(jnp.sum(inside * (prefix[here] + base), axis=0, keepdims=True))
        base = base + totals[here]
    rank = jnp.concatenate(ranks, 1)
    rank_ref[...] = rank
    at_rank = chosen(equal_rows(rank, CAP), jnp.ones((1, S_DEV), F32))
    for copy in copies[1:]:
        copy.wait()
    place = (cell_v[...] * 256 + offset_v[...]).astype(F32)
    dose = dose_v[...]
    parts = [chosen(mine, part) for part in split3(place) + split3(dose)]
    packed = nt_dot(jnp.concatenate(parts, 0), at_rank)
    for which in range(2):
        p = packed[3 * which * N_ROW:3 * (which + 1) * N_ROW]
        whole = p[:N_ROW] + p[N_ROW:2 * N_ROW] + p[2 * N_ROW:]
        for t in range(NT):
            start = (2 * t + which) * CAP
            send_ref[:, 0, start:start + CAP] = shifted_rows(whole, t - REACH)


def decoded(place):
    cell = jnp.floor(place * (1.0 / 256.0))
    fine = place - 256.0 * cell
    cell_y = jnp.floor((cell + 0.5) * (1.0 / (CX - 1)))
    cell_x = cell - (CX - 1) * cell_y
    off_y = jnp.floor(fine * (1.0 / 16.0))
    off_x = fine - 16.0 * off_y
    block = jnp.floor(cell_x * (1.0 / BLK))
    column = cell_x - BLK * block
    off_y, off_x = off_y * (1.0 / 16.0), off_x * (1.0 / 16.0)
    return dict(block=block, y=cell_y, y1=cell_y + 1.0, column=column, column1=column + 1.0,
                y0w=1.0 - off_y, y1w=off_y, x0=1.0 - off_x, x1=off_x)


def pair_columns(shot, i):
    return jnp.concatenate([column_chunk(shot, i), column_chunk(shot, i + 1)], 1)


def over_rows(v, i):
    return jnp.broadcast_to(v[i:i + 1], (SUB16, CAP)).astype(BF)


def row_numbers(first):
    return (lax.broadcasted_iota(jnp.int32, (SUB16, CAP), 0) + first).astype(F32).astype(BF)


def column_chunk(shot, i):
    first, second = over_rows(shot["column"], i), over_rows(shot["column1"], i)
    w0, w1 = over_rows(shot["x0"], i), over_rows(shot["x1"], i)
    none = jnp.zeros_like(w0)
    out = []
    for k in range(XR // SUB16):
        at = row_numbers(SUB16 * k)
        out.append(jnp.where(at == first, w0, jnp.where(at == second, w1, none)))
    return jnp.concatenate(out, 0)


def row_chunk(shot, dosed, i, at_dosed):
    first, second = over_rows(shot["y"], i), over_rows(shot["y1"], i)
    block = over_rows(shot["block"], i)
    values = [over_rows(v, at_dosed) for v in dosed]
    none = jnp.zeros_like(first)
    parts = [[], []]
    for k in range(CY // SUB16):
        at = row_numbers(SUB16 * k)
        on_first, on_second = at == first, at == second
        for part in range(2):
            q0, q1 = values[2 * part:2 * part + 2]
            parts[part].append(jnp.where(on_first, q0, jnp.where(on_second, q1, none)))
    inside = [block == jnp.full((SUB16, CAP), h, F32).astype(BF) for h in range(NB)]
    return jnp.concatenate([jnp.where(inside[h], v, none) for part in parts for h in range(NB) for v in part], 0)


def dosed_weights(shot, dose, sources=slice(None)):
    hi0, lo0 = split2(shot["y0w"][sources] * dose)
    hi1, lo1 = split2(shot["y1w"][sources] * dose)
    return [v.astype(F32) for v in (hi0, hi1, lo0, lo1)]


def density_pair(shot, dosed, first, i, columns):
    a = jnp.concatenate([row_chunk(shot, dosed, j, j - first) for j in (i, i + 1)], 1)
    return nt_dot(a, columns)


def assembled(both):
    d = both[:BLK] + both[BLK:]
    blocks = [d[:CY, :BLK]]
    for h in range(1, NB):
        over = d[(h - 1) * CY:h * CY, BLK:XR]
        over = jnp.concatenate([over, jnp.zeros((CY, BLK - XR + BLK), F32)], 1)
        blocks.append(d[h * CY:(h + 1) * CY, :BLK] + over)
    return jnp.concatenate(blocks, 1)


def added(total, one):
    return one if total is None else total + one


def tile_density(shot, dose):
    dosed = dosed_weights(shot, dose)
    both = None
    for i in range(0, N_ROW, 2):
        both = added(both, density_pair(shot, dosed, 0, i, pair_columns(shot, i)))
    return assembled(both)


def packed_edge(block, lane0):
    rows = block.shape[0] // 4
    lane = lax.broadcasted_iota(jnp.int32, (rows, BLK), 1)
    out = jnp.zeros((rows, BLK), block.dtype)
    for g in range(4):
        part = block[g * rows:(g + 1) * rows]
        shift = (32 * g - lane0) % BLK
        part = pltpu.roll(part, shift, 1) if shift else part
        out = jnp.where(lane // 32 == g, part, out)
    return out


def unpacked_edge(edge, lane0):
    parts = []
    for g in range(4):
        shift = (lane0 - 32 * g) % BLK
        parts.append(pltpu.roll(edge, shift, 1) if shift else edge)
    return jnp.concatenate(parts, 0)


def blurred_y(density, taps_ref):
    hi, lo = split2(density)
    both = nn_dot(taps_ref[...], jnp.concatenate([hi, lo], 0))
    rows = both.shape[0] // 2
    return both[:rows] + both[rows:]


def edge_products(stacked, taps):
    both = nn_dot(jnp.concatenate(split2(stacked), 0), taps)
    rows = stacked.shape[0]
    both = both[:rows] + both[rows:]
    return both[:, :BLK] + both[:, BLK:]


def blurred_inside(along_y, taps_ref):
    none = jnp.zeros((along_y.shape[0], BLK), F32)
    wide = jnp.concatenate([none, along_y, none], 1)
    rows = along_y.shape[0]
    out = edge_products(jnp.concatenate([wide[:, h * BLK:(h + 3) * BLK] for h in range(NB)], 0), taps_ref[...])
    return jnp.concatenate([out[h * rows:(h + 1) * rows] for h in range(NB)], 1)


def blurred_sides(from_left_ref, from_right_ref, taps_ref):
    col = lax.axis_index("col")
    left = unpacked_edge(jnp.where(col > 0, from_left_ref[...], 0.0), BLK - 32)
    right = unpacked_edge(jnp.where(col < N_COL - 1, from_right_ref[...], 0.0), 0)
    return edge_products(left, taps_ref[:BLK]), edge_products(right, taps_ref[2 * BLK:])


def gather_table(total):
    pieces = []
    for h in range(NB):
        inside = total[:, h * BLK:(h + 1) * BLK]
        if h + 1 < NB:
            after = total[:, (h + 1) * BLK:(h + 1) * BLK + XR - BLK]
        else:
            after = jnp.zeros((CY, XR - BLK), F32)
        pieces.append(jnp.concatenate([inside, after], 1))
    return jnp.concatenate(split2(jnp.concatenate(pieces, 0)), 0)


def gather_pair(table, shot, i, columns):
    both = nn_dot(table, columns)
    at = lax.broadcasted_iota(jnp.int32, (CY, CAP), 0).astype(F32)
    rows = []
    for j in range(2):
        here = slice(j * CAP, (j + 1) * CAP)
        g = both[:BLK, here] + both[BLK:, here]
        block, y, y1, w0, w1 = (shot[name][i + j:i + j + 1] for name in ("block", "y", "y1", "y0w", "y1w"))
        mine = g[:CY]
        for h in range(1, NB):
            mine = jnp.where(block == float(h), g[h * CY:(h + 1) * CY], mine)
        w = jnp.where(at == y, w0, jnp.where(at == y1, w1, 0.0))
        rows.append(jnp.sum(w * mine, axis=0, keepdims=True))
    return rows


def corrected(dose, exposure):
    return jnp.where(dose > 0.0, dose * (1.0 + BACKSCATTER) / exposure, 0.0)


def slots(recv_ref, t):
    start = 2 * t * CAP
    return recv_ref[:, 0, start:start + CAP], recv_ref[:, 0, start + CAP:start + 2 * CAP]


def first_kernel(recv_ref, ltaps_ref, along_ref, density_ref, to_left_ref, to_right_ref):
    tiles = []
    for t in range(NT):
        place, dose = slots(recv_ref, t)
        shot = decoded(place)
        tiles.append(tile_density(shot, dose))
    density_ref[...] = jnp.concatenate(tiles[1:NT - 1], 0)
    along = blurred_y(jnp.concatenate(tiles, 0), ltaps_ref)
    along_ref[...] = along
    to_left_ref[...] = packed_edge(along[:, :BLK], 0)
    to_right_ref[...] = packed_edge(along[:, CX - BLK:], BLK - 32)


def inside_kernel(along_ref, rtaps_ref, field_ref):
    field_ref[...] = blurred_inside(along_ref[...], rtaps_ref)


def full_field(inside_ref, from_left_ref, from_right_ref, rtaps_ref):
    left, right = blurred_sides(from_left_ref, from_right_ref, rtaps_ref)
    return jnp.concatenate(
        [inside_ref[:, :BLK] + left, inside_ref[:, BLK:CX - BLK], inside_ref[:, CX - BLK:] + right], 1)


def second_kernel(recv_ref, inside_ref, density_ref, from_left_ref, from_right_ref, rtaps_ref, ltaps_ref,
                  dose_ref, along2_ref, density2_ref, to_left_ref, to_right_ref, b_ref):
    total = density_ref[...] + BACKSCATTER * full_field(inside_ref, from_left_ref, from_right_ref, rtaps_ref)
    places = [slots(recv_ref, n + 1) for n in range(NT - 2)]
    shots = [decoded(place) for place, _ in places]
    tables = [gather_table(total[n * CY:(n + 1) * CY]) for n in range(NT - 2)]
    densities = [None] * (NT - 2)
    groups = [(n, first) for n in range(NT - 2) for first in range(0, N_ROW, GROUP)]
    dosed = None
    for step in range(len(groups) + 1):
        rows = []
        for j in range(0, GROUP, 2):
            if step < len(groups):
                n, first = groups[step]
                columns = pair_columns(shots[n], first + j)
                b_ref[n, :, (first + j) * CAP:(first + j + 2) * CAP] = columns
                rows += gather_pair(tables[n], shots[n], first + j, columns)
            if step > 0:
                m, start = groups[step - 1]
                columns = b_ref[m, :, (start + j) * CAP:(start + j + 2) * CAP]
                densities[m] = added(densities[m], density_pair(shots[m], dosed, start, start + j, columns))
        if rows:
            sources = slice(first, first + GROUP)
            dose = corrected(places[n][1][sources], jnp.concatenate(rows, 0))
            if n + 1 == REACH:
                dose_ref[sources, :] = dose
            dosed = dosed_weights(shots[n], dose, sources)
    tiles = [assembled(both) for both in densities]
    density2_ref[...] = tiles[1]
    along = blurred_y(jnp.concatenate(tiles, 0), ltaps_ref)
    along2_ref[...] = along
    to_left_ref[...] = packed_edge(along[:, :BLK], 0)
    to_right_ref[...] = packed_edge(along[:, CX - BLK:], BLK - 32)


def third_kernel(recv_ref, dose_ref, inside_ref, density_ref, from_left_ref, from_right_ref, rtaps_ref, field_hbm, final_ref,
                 field_ref, sem):
    field = full_field(inside_ref, from_left_ref, from_right_ref, rtaps_ref)
    field_ref[...] = field
    copy = pltpu.make_async_copy(field_ref, field_hbm, sem)
    copy.start()
    shot = decoded(slots(recv_ref, REACH)[0])
    table = gather_table(density_ref[...] + BACKSCATTER * field)
    rows = []
    for i in range(0, N_ROW, 2):
        rows += gather_pair(table, shot, i, pair_columns(shot, i))
    final_ref[:, 0, :] = corrected(dose_ref[...], jnp.concatenate(rows, 0))
    copy.wait()


def unpack_kernel(ret_ref, owner_ref, rank_ref, out_ref):
    at_rank = chosen(equal_rows(rank_ref[...], CAP), jnp.ones((1, S_DEV), F32))
    parts = jnp.concatenate([p.astype(BF) for p in split3(ret_ref[:, 0, :])], 0)
    g = nn_dot(parts, at_rank)
    whole = g[:N_ROW] + g[N_ROW:2 * N_ROW] + g[2 * N_ROW:]
    mine = owner_ref[...] == lax.broadcasted_iota(jnp.int32, (N_ROW, S_DEV), 0).astype(F32)
    out_ref[...] = jnp.sum(jnp.where(mine, whole, 0.0), axis=0, keepdims=True)


def call(kernel, outs, n_in, scratch=(), space=pltpu.VMEM, out_spaces=None):
    return pl.pallas_call(
        kernel,
        out_shape=[jax.ShapeDtypeStruct(s, F32) for s in outs],
        in_specs=[pl.BlockSpec(memory_space=space)] * n_in,
        out_specs=[pl.BlockSpec(memory_space=s) for s in out_spaces or [pltpu.VMEM] * len(outs)],
        scratch_shapes=list(scratch),
        compiler_params=pltpu.CompilerParams(vmem_limit_bytes=48 << 20),
    )


def exchanged(to_left, to_right):
    n = lax.axis_size("col")
    from_left = lax.ppermute(to_right, "col", [(i, (i + 1) % n) for i in range(n)])
    from_right = lax.ppermute(to_left, "col", [((i + 1) % n, i) for i in range(n)])
    return from_left, from_right


def per_device(shot_dose, shot_owner, shot_cell, shot_offset):
    ltaps = jnp.asarray(left_constant(3 * CY, NT * CY, CY))
    ltaps2 = jnp.asarray(left_constant(CY, 3 * CY, CY))
    rtaps = jnp.asarray(right_constant())
    row = (1, S_DEV)
    rows = [pltpu.VMEM(row, F32)] + [pltpu.VMEM(row, jnp.int32)] * 3 + [pltpu.SemaphoreType.DMA((4,))]
    send, rank, owner = call(pack_kernel, [(N_ROW, 1, 2 * NT * CAP), row, row], 4, rows, pltpu.HBM)(
        *(pltpu.with_memory_space_constraint(v.reshape(row), pltpu.HBM) for v in (shot_dose, shot_owner, shot_cell, shot_offset))
    )
    recv = lax.all_to_all(send, "row", split_axis=0, concat_axis=0, tiled=True)
    edge = (3 * CY // 4, BLK)
    along, density, to_left, to_right = call(first_kernel, [(3 * CY, CX), (3 * CY, CX), edge, edge], 2)(recv, ltaps)
    from_left, from_right = exchanged(to_left, to_right)
    (inside,) = call(inside_kernel, [(3 * CY, CX)], 2)(along, rtaps)
    edge = (CY // 4, BLK)
    dose, along, density, to_left, to_right = call(
        second_kernel, [(N_ROW, CAP), (CY, CX), (CY, CX), edge, edge], 7, (pltpu.VMEM((NT - 2, XR, SLOTS), BF),)
    )(recv, inside, density, from_left, from_right, rtaps, ltaps2)
    from_left, from_right = exchanged(to_left, to_right)
    (inside,) = call(inside_kernel, [(CY, CX)], 2)(along, rtaps)
    field, final = call(
        third_kernel, [(CY, CX), (N_ROW, 1, CAP)], 7, (pltpu.VMEM((CY, CX), F32), pltpu.SemaphoreType.DMA),
        out_spaces=[pltpu.HBM, pltpu.VMEM],
    )(
        recv, dose, inside, density, from_left, from_right, rtaps
    )
    back = lax.all_to_all(final, "row", split_axis=0, concat_axis=0, tiled=True)
    (out,) = call(unpack_kernel, [(1, S_DEV)], 3)(back, owner, rank)
    return out.reshape(S_DEV), field


def solution(mesh):
    placed = (P(("row", "col")), P(("row", "col"), None), P(("row", "col")), P(("row", "col")))
    return jax.shard_map(
        per_device,
        mesh=mesh,
        in_specs=placed,
        out_specs=(P(("row", "col")), P("row", "col")),
        check_vma=False,
    )
```

```python
import jax
import jax.numpy as jnp
import numpy as np
from jax import lax
from jax.experimental import pallas as pl
from jax.experimental.pallas import tpu as pltpu
from jax.sharding import PartitionSpec as P

CY = 32
CX = 512
HALF = 30
N_ROW = 32
N_COL = 8
S_DEV = 2048
CAP = 128
REACH = 2
NT = 2 * REACH + 1
BLK = 128
NB = CX // BLK
XR = BLK + 16
SLOTS = N_ROW * CAP
GROUP = 8
SUB16 = 16
BF = jnp.bfloat16
F32 = jnp.float32

BACKSCATTER = 0.6
SPREAD = 10.0


def taps():
    lags = np.arange(2 * HALF + 1, dtype=np.float64) - HALF
    values = np.exp(-(lags * lags) / (2.0 * SPREAD * SPREAD))
    return values / values.sum()


def band(rows, cols, offset):
    lag = np.arange(cols)[None, :] - np.arange(rows)[:, None] - offset + HALF
    t = taps()
    return np.where((lag >= 0) & (lag <= 2 * HALF), t[np.clip(lag, 0, 2 * HALF)], 0.0)


def two(m):
    hi = m.astype(jnp.bfloat16)
    lo = (m - hi.astype(np.float64)).astype(jnp.bfloat16)
    return np.asarray(hi), np.asarray(lo)


def left_constant(rows, cols, offset):
    hi, lo = two(band(rows, cols, offset))
    tiles = [slice(n, n + CY) for n in range(0, cols, CY)]
    return np.stack([np.concatenate([np.concatenate([m[:, n], m[:, n]], 1) for m in (hi, lo)], 0) for n in tiles])


def right_constant():
    hi, lo = two(band(BLK, 3 * BLK, BLK).T)
    return np.concatenate([hi, lo], 1)


def split2(v):
    hi = v.astype(BF)
    lo = (v - hi.astype(F32)).astype(BF)
    return hi, lo


def split3(v):
    hi = v.astype(BF).astype(F32)
    rest = v - hi
    mid = rest.astype(BF).astype(F32)
    return hi, mid, rest - mid


def nt_dot(a, b):
    return lax.dot_general(a, b, (((1,), (1,)), ((), ())), preferred_element_type=F32)


def nn_dot(a, b):
    return lax.dot_general(a, b, (((1,), (0,)), ((), ())), preferred_element_type=F32)


def shifted_rows(v, by):
    if by == 0:
        return v
    pad = jnp.zeros((abs(by), v.shape[1]), v.dtype)
    return jnp.concatenate([v[by:], pad], 0) if by > 0 else jnp.concatenate([pad, v[:by]], 0)


def repeated(row):
    return jnp.broadcast_to(row, (SUB16, row.shape[1])).astype(BF)


def numbers(first, width):
    return (lax.broadcasted_iota(jnp.int32, (SUB16, width), 0) + first).astype(F32).astype(BF)


def equal_rows(row, rows):
    wide = repeated(row)
    return [numbers(SUB16 * k, row.shape[1]) == wide for k in range(rows // SUB16)]


def chosen(masks, row):
    wide = repeated(row)
    none = jnp.zeros_like(wide)
    return jnp.concatenate([jnp.where(m, wide, none) for m in masks], 0)


def pack_kernel(dose_hbm, owner_hbm, cell_hbm, offset_hbm, send_ref, rank_ref, owner_ref,
                dose_v, owner_v, cell_v, offset_v, sems):
    copies = [pltpu.make_async_copy(src, dst, sems.at[n]) for n, (src, dst) in enumerate(
        ((owner_hbm, owner_v), (cell_hbm, cell_v), (offset_hbm, offset_v), (dose_hbm, dose_v)))]
    for copy in copies:
        copy.start()
    chunk = 256
    n_chunks = S_DEV // chunk
    rows_at = lax.broadcasted_iota(jnp.int32, (chunk, chunk), 0)
    cols_at = lax.broadcasted_iota(jnp.int32, (chunk, chunk), 1)
    before = jnp.where(rows_at < cols_at, 1.0, 0.0).astype(BF)
    copies[0].wait()
    owner = owner_v[...].astype(F32)
    owner_ref[...] = owner
    mine = equal_rows(owner, N_ROW)
    ones = chosen(mine, jnp.ones((1, S_DEV), F32))
    stacked = jnp.concatenate([ones[:, c * chunk:(c + 1) * chunk] for c in range(n_chunks)], 0)
    prefix = nn_dot(stacked, before)
    totals = prefix[:, chunk - 1:] + stacked[:, chunk - 1:].astype(F32)
    base = jnp.zeros((N_ROW, 1), F32)
    ranks = []
    for c in range(n_chunks):
        here = slice(c * N_ROW, (c + 1) * N_ROW)
        inside = ones[:, c * chunk:(c + 1) * chunk].astype(F32)
        ranks.append(jnp.sum(inside * (prefix[here] + base), axis=0, keepdims=True))
        base = base + totals[here]
    rank = jnp.concatenate(ranks, 1)
    rank_ref[...] = rank
    at_rank = chosen(equal_rows(rank, CAP), jnp.ones((1, S_DEV), F32))
    for copy in copies[1:]:
        copy.wait()
    place = (cell_v[...] * 256 + offset_v[...]).astype(F32)
    dose = dose_v[...]
    parts = [chosen(mine, part) for part in split3(place) + split3(dose)]
    packed = nt_dot(jnp.concatenate(parts, 0), at_rank)
    for which in range(2):
        p = packed[3 * which * N_ROW:3 * (which + 1) * N_ROW]
        whole = p[:N_ROW] + p[N_ROW:2 * N_ROW] + p[2 * N_ROW:]
        for t in range(NT):
            start = (2 * t + which) * CAP
            send_ref[:, 0, start:start + CAP] = shifted_rows(whole, t - REACH)


def decoded(place):
    cell = jnp.floor(place * (1.0 / 256.0))
    fine = place - 256.0 * cell
    cell_y = jnp.floor((cell + 0.5) * (1.0 / (CX - 1)))
    cell_x = cell - (CX - 1) * cell_y
    off_y = jnp.floor(fine * (1.0 / 16.0))
    off_x = fine - 16.0 * off_y
    block = jnp.floor(cell_x * (1.0 / BLK))
    column = cell_x - BLK * block
    off_y, off_x = off_y * (1.0 / 16.0), off_x * (1.0 / 16.0)
    return dict(block=block, y=cell_y, y1=cell_y + 1.0, column=column, column1=column + 1.0,
                y0w=1.0 - off_y, y1w=off_y, x0=1.0 - off_x, x1=off_x)


def pair_columns(shot, i):
    return jnp.concatenate([column_chunk(shot, i), column_chunk(shot, i + 1)], 1)


def over_rows(v, i):
    return jnp.broadcast_to(v[i:i + 1], (SUB16, CAP)).astype(BF)


def row_numbers(first):
    return (lax.broadcasted_iota(jnp.int32, (SUB16, CAP), 0) + first).astype(F32).astype(BF)


def column_chunk(shot, i):
    first, w1 = over_rows(shot["column"], i), over_rows(shot["x1"], i)
    second, w0 = first + jnp.ones_like(first), jnp.ones_like(w1) - w1
    none = jnp.zeros_like(w0)
    out = []
    for k in range(XR // SUB16):
        at = row_numbers(SUB16 * k)
        out.append(jnp.where(at == first, w0, jnp.where(at == second, w1, none)))
    return jnp.concatenate(out, 0)


def row_chunk(shot, dosed, i, at_dosed):
    first = over_rows(shot["y"], i)
    second = first + jnp.ones_like(first)
    block = over_rows(shot["block"], i)
    values = [over_rows(v, at_dosed) for v in dosed]
    none = jnp.zeros_like(first)
    parts = [[], []]
    for k in range(CY // SUB16):
        at = row_numbers(SUB16 * k)
        on_first, on_second = at == first, at == second
        for part in range(2):
            q0, q1 = values[2 * part:2 * part + 2]
            parts[part].append(jnp.where(on_first, q0, jnp.where(on_second, q1, none)))
    inside = [block == jnp.full((SUB16, CAP), h, F32).astype(BF) for h in range(NB)]
    return jnp.concatenate([jnp.where(inside[h], v, none) for part in parts for h in range(NB) for v in part], 0)


def dosed_weights(shot, dose, sources=slice(None)):
    hi0, lo0 = split2(shot["y0w"][sources] * dose)
    hi1, lo1 = split2(shot["y1w"][sources] * dose)
    return [v.astype(F32) for v in (hi0, hi1, lo0, lo1)]


def density_pair(shot, dosed, first, i, columns):
    a = jnp.concatenate([row_chunk(shot, dosed, j, j - first) for j in (i, i + 1)], 1)
    return nt_dot(a, columns)


def assembled(both):
    d = both[:BLK] + both[BLK:]
    blocks = [d[:CY, :BLK]]
    for h in range(1, NB):
        over = d[(h - 1) * CY:h * CY, BLK:XR]
        over = jnp.concatenate([over, jnp.zeros((CY, BLK - XR + BLK), F32)], 1)
        blocks.append(d[h * CY:(h + 1) * CY, :BLK] + over)
    return jnp.concatenate(blocks, 1)


def added(total, one):
    return one if total is None else total + one


def tile_density(shot, dose):
    dosed = dosed_weights(shot, dose)
    both = None
    for i in range(0, N_ROW, 2):
        both = added(both, density_pair(shot, dosed, 0, i, pair_columns(shot, i)))
    return assembled(both)


def packed_edge(block, lane0):
    rows = block.shape[0] // 4
    lane = lax.broadcasted_iota(jnp.int32, (rows, BLK), 1)
    out = jnp.zeros((rows, BLK), block.dtype)
    for g in range(4):
        part = block[g * rows:(g + 1) * rows]
        shift = (32 * g - lane0) % BLK
        part = pltpu.roll(part, shift, 1) if shift else part
        out = jnp.where(lane // 32 == g, part, out)
    return out


def unpacked_edge(edge, lane0):
    parts = []
    for g in range(4):
        shift = (lane0 - 32 * g) % BLK
        parts.append(pltpu.roll(edge, shift, 1) if shift else edge)
    return jnp.concatenate(parts, 0)


def blurred_y(tiles, taps_ref):
    both = None
    for n, density in enumerate(tiles):
        both = added(both, nn_dot(taps_ref[n], jnp.concatenate(split2(density), 0)))
    rows = both.shape[0] // 2
    return both[:rows] + both[rows:]


def edge_products(stacked, taps):
    both = nn_dot(jnp.concatenate(split2(stacked), 0), taps)
    rows = stacked.shape[0]
    both = both[:rows] + both[rows:]
    return both[:, :BLK] + both[:, BLK:]


def blurred_inside(along_y, taps_ref):
    none = jnp.zeros((along_y.shape[0], BLK), F32)
    wide = jnp.concatenate([none, along_y, none], 1)
    rows = along_y.shape[0]
    out = edge_products(jnp.concatenate([wide[:, h * BLK:(h + 3) * BLK] for h in range(NB)], 0), taps_ref[...])
    return jnp.concatenate([out[h * rows:(h + 1) * rows] for h in range(NB)], 1)


def blurred_sides(from_left_ref, from_right_ref, taps_ref):
    col = lax.axis_index("col")
    left = unpacked_edge(jnp.where(col > 0, from_left_ref[...], 0.0), BLK - 32)
    right = unpacked_edge(jnp.where(col < N_COL - 1, from_right_ref[...], 0.0), 0)
    return edge_products(left, taps_ref[:BLK]), edge_products(right, taps_ref[2 * BLK:])


def gather_table(total):
    pieces = []
    for h in range(NB):
        inside = total[:, h * BLK:(h + 1) * BLK]
        if h + 1 < NB:
            after = total[:, (h + 1) * BLK:(h + 1) * BLK + XR - BLK]
        else:
            after = jnp.zeros((CY, XR - BLK), F32)
        pieces.append(jnp.concatenate([inside, after], 1))
    return jnp.concatenate(split2(jnp.concatenate(pieces, 0)), 0)


def gather_pair(table, shot, i, columns):
    both = nn_dot(table, columns)
    at = lax.broadcasted_iota(jnp.int32, (CY, CAP), 0).astype(F32)
    rows = []
    for j in range(2):
        here = slice(j * CAP, (j + 1) * CAP)
        g = both[:BLK, here] + both[BLK:, here]
        block, y, w1 = (jnp.broadcast_to(shot[name][i + j:i + j + 1], (8, CAP)) for name in ("block", "y", "y1w"))
        block, y, w1, y1, w0 = (jnp.concatenate([v] * (CY // 8), 0) for v in (block, y, w1, y + 1.0, 1.0 - w1))
        mine = g[:CY]
        for h in range(1, NB):
            mine = jnp.where(block == float(h), g[h * CY:(h + 1) * CY], mine)
        w = jnp.where(at == y, w0, jnp.where(at == y1, w1, 0.0))
        rows.append(jnp.sum(w * mine, axis=0, keepdims=True))
    return rows


def corrected(dose, exposure):
    return jnp.where(dose > 0.0, dose * (1.0 + BACKSCATTER) / exposure, 0.0)


def slots(recv_ref, t):
    start = 2 * t * CAP
    return recv_ref[:, 0, start:start + CAP], recv_ref[:, 0, start + CAP:start + 2 * CAP]


def first_kernel(recv_ref, ltaps_ref, along_ref, density_ref, to_left_ref, to_right_ref):
    tiles = []
    for t in range(NT):
        place, dose = slots(recv_ref, t)
        shot = decoded(place)
        tiles.append(tile_density(shot, dose))
    density_ref[...] = jnp.concatenate(tiles[1:NT - 1], 0)
    along = blurred_y(tiles, ltaps_ref)
    along_ref[...] = along
    to_left_ref[...] = packed_edge(along[:, :BLK], 0)
    to_right_ref[...] = packed_edge(along[:, CX - BLK:], BLK - 32)


def inside_kernel(along_ref, rtaps_ref, field_ref):
    field_ref[...] = blurred_inside(along_ref[...], rtaps_ref)


def full_field(inside_ref, from_left_ref, from_right_ref, rtaps_ref):
    left, right = blurred_sides(from_left_ref, from_right_ref, rtaps_ref)
    return jnp.concatenate(
        [inside_ref[:, :BLK] + left, inside_ref[:, BLK:CX - BLK], inside_ref[:, CX - BLK:] + right], 1)


def second_kernel(recv_ref, inside_ref, density_ref, from_left_ref, from_right_ref, rtaps_ref, ltaps_ref,
                  dose_ref, along2_ref, density2_ref, to_left_ref, to_right_ref, b_ref):
    total = density_ref[...] + BACKSCATTER * full_field(inside_ref, from_left_ref, from_right_ref, rtaps_ref)
    places = [slots(recv_ref, n + 1) for n in range(NT - 2)]
    shots = [decoded(place) for place, _ in places]
    tables = [gather_table(total[n * CY:(n + 1) * CY]) for n in range(NT - 2)]
    densities = [None] * (NT - 2)
    groups = [(n, first) for n in range(NT - 2) for first in range(0, N_ROW, GROUP)]
    dosed = None
    for step in range(len(groups) + 1):
        rows = []
        for j in range(0, GROUP, 2):
            if step < len(groups):
                n, first = groups[step]
                columns = pair_columns(shots[n], first + j)
                b_ref[n, :, (first + j) * CAP:(first + j + 2) * CAP] = columns
                rows += gather_pair(tables[n], shots[n], first + j, columns)
            if step > 0:
                m, start = groups[step - 1]
                columns = b_ref[m, :, (start + j) * CAP:(start + j + 2) * CAP]
                densities[m] = added(densities[m], density_pair(shots[m], dosed, start, start + j, columns))
        if rows:
            sources = slice(first, first + GROUP)
            dose = corrected(places[n][1][sources], jnp.concatenate(rows, 0))
            if n + 1 == REACH:
                dose_ref[sources, :] = dose
            dosed = dosed_weights(shots[n], dose, sources)
    tiles = [assembled(both) for both in densities]
    density2_ref[...] = tiles[1]
    along = blurred_y(tiles, ltaps_ref)
    along2_ref[...] = along
    to_left_ref[...] = packed_edge(along[:, :BLK], 0)
    to_right_ref[...] = packed_edge(along[:, CX - BLK:], BLK - 32)


def third_kernel(recv_ref, dose_ref, inside_ref, density_ref, from_left_ref, from_right_ref, rtaps_ref, field_hbm, final_ref,
                 field_ref, sem):
    field = full_field(inside_ref, from_left_ref, from_right_ref, rtaps_ref)
    field_ref[...] = field
    copy = pltpu.make_async_copy(field_ref, field_hbm, sem)
    copy.start()
    shot = decoded(slots(recv_ref, REACH)[0])
    table = gather_table(density_ref[...] + BACKSCATTER * field)
    rows = []
    for i in range(0, N_ROW, 2):
        rows += gather_pair(table, shot, i, pair_columns(shot, i))
    final_ref[:, 0, :] = corrected(dose_ref[...], jnp.concatenate(rows, 0))
    copy.wait()


def unpack_kernel(ret_ref, owner_ref, rank_ref, out_ref):
    at_rank = chosen(equal_rows(rank_ref[...], CAP), jnp.ones((1, S_DEV), F32))
    parts = jnp.concatenate([p.astype(BF) for p in split3(ret_ref[:, 0, :])], 0)
    g = nn_dot(parts, at_rank)
    whole = g[:N_ROW] + g[N_ROW:2 * N_ROW] + g[2 * N_ROW:]
    mine = owner_ref[...] == lax.broadcasted_iota(jnp.int32, (N_ROW, S_DEV), 0).astype(F32)
    out_ref[...] = jnp.sum(jnp.where(mine, whole, 0.0), axis=0, keepdims=True)


def call(kernel, outs, n_in, scratch=(), space=pltpu.VMEM, out_spaces=None):
    return pl.pallas_call(
        kernel,
        out_shape=[jax.ShapeDtypeStruct(s, F32) for s in outs],
        in_specs=[pl.BlockSpec(memory_space=space)] * n_in,
        out_specs=[pl.BlockSpec(memory_space=s) for s in out_spaces or [pltpu.VMEM] * len(outs)],
        scratch_shapes=list(scratch),
        compiler_params=pltpu.CompilerParams(vmem_limit_bytes=48 << 20),
    )


def exchanged(to_left, to_right):
    n = lax.axis_size("col")
    from_left = lax.ppermute(to_right, "col", [(i, (i + 1) % n) for i in range(n)])
    from_right = lax.ppermute(to_left, "col", [((i + 1) % n, i) for i in range(n)])
    return from_left, from_right


def per_device(shot_dose, shot_owner, shot_cell, shot_offset):
    ltaps = jnp.asarray(left_constant(3 * CY, NT * CY, CY))
    ltaps2 = jnp.asarray(left_constant(CY, 3 * CY, CY))
    rtaps = jnp.asarray(right_constant())
    row = (1, S_DEV)
    rows = [pltpu.VMEM(row, F32)] + [pltpu.VMEM(row, jnp.int32)] * 3 + [pltpu.SemaphoreType.DMA((4,))]
    send, rank, owner = call(pack_kernel, [(N_ROW, 1, 2 * NT * CAP), row, row], 4, rows, pltpu.HBM)(
        *(pltpu.with_memory_space_constraint(v.reshape(row), pltpu.HBM) for v in (shot_dose, shot_owner, shot_cell, shot_offset))
    )
    recv = lax.all_to_all(send, "row", split_axis=0, concat_axis=0, tiled=True)
    edge = (3 * CY // 4, BLK)
    along, density, to_left, to_right = call(first_kernel, [(3 * CY, CX), (3 * CY, CX), edge, edge], 2)(recv, ltaps)
    from_left, from_right = exchanged(to_left, to_right)
    (inside,) = call(inside_kernel, [(3 * CY, CX)], 2)(along, rtaps)
    edge = (CY // 4, BLK)
    dose, along, density, to_left, to_right = call(
        second_kernel, [(N_ROW, CAP), (CY, CX), (CY, CX), edge, edge], 7, (pltpu.VMEM((NT - 2, XR, SLOTS), BF),)
    )(recv, inside, density, from_left, from_right, rtaps, ltaps2)
    from_left, from_right = exchanged(to_left, to_right)
    (inside,) = call(inside_kernel, [(CY, CX)], 2)(along, rtaps)
    field, final = call(
        third_kernel, [(CY, CX), (N_ROW, 1, CAP)], 7, (pltpu.VMEM((CY, CX), F32), pltpu.SemaphoreType.DMA),
        out_spaces=[pltpu.HBM, pltpu.VMEM],
    )(
        recv, dose, inside, density, from_left, from_right, rtaps
    )
    back = lax.all_to_all(final, "row", split_axis=0, concat_axis=0, tiled=True)
    (out,) = call(unpack_kernel, [(1, S_DEV)], 3)(back, owner, rank)
    return out.reshape(S_DEV), field


def solution(mesh):
    placed = (P(("row", "col")), P(("row", "col"), None), P(("row", "col")), P(("row", "col")))
    return jax.shard_map(
        per_device,
        mesh=mesh,
        in_specs=placed,
        out_specs=(P(("row", "col")), P("row", "col")),
        check_vma=False,
    )
```

```python
import jax
import jax.numpy as jnp
import numpy as np
from jax import lax
from jax.experimental import pallas as pl
from jax.experimental.pallas import tpu as pltpu
from jax.sharding import PartitionSpec as P

CY = 32
CX = 512
HALF = 30
N_ROW = 32
N_COL = 8
S_DEV = 2048
CAP = 128
REACH = 2
NT = 2 * REACH + 1
BLK = 128
NB = CX // BLK
XR = BLK + 16
SLOTS = N_ROW * CAP
GROUP = 8
SUB16 = 16
BF = jnp.bfloat16
F32 = jnp.float32

BACKSCATTER = 0.6
SPREAD = 10.0


def taps():
    lags = np.arange(2 * HALF + 1, dtype=np.float64) - HALF
    values = np.exp(-(lags * lags) / (2.0 * SPREAD * SPREAD))
    return values / values.sum()


def band(rows, cols, offset):
    lag = np.arange(cols)[None, :] - np.arange(rows)[:, None] - offset + HALF
    t = taps()
    return np.where((lag >= 0) & (lag <= 2 * HALF), t[np.clip(lag, 0, 2 * HALF)], 0.0)


def two(m):
    hi = m.astype(jnp.bfloat16)
    lo = (m - hi.astype(np.float64)).astype(jnp.bfloat16)
    return np.asarray(hi), np.asarray(lo)


def left_constant(rows, cols, offset):
    hi, lo = two(band(rows, cols, offset))
    tiles = [slice(n, n + CY) for n in range(0, cols, CY)]
    return np.stack([np.concatenate([np.concatenate([m[:, n], m[:, n]], 1) for m in (hi, lo)], 0) for n in tiles])


def right_constant():
    hi, lo = two(band(BLK, 3 * BLK, BLK).T)
    return np.concatenate([hi, lo], 1)


def split2(v):
    hi = v.astype(BF)
    lo = (v - hi.astype(F32)).astype(BF)
    return hi, lo


def split3(v):
    hi = v.astype(BF).astype(F32)
    rest = v - hi
    mid = rest.astype(BF).astype(F32)
    return hi, mid, rest - mid


def nt_dot(a, b):
    return lax.dot_general(a, b, (((1,), (1,)), ((), ())), preferred_element_type=F32)


def nn_dot(a, b):
    return lax.dot_general(a, b, (((1,), (0,)), ((), ())), preferred_element_type=F32)


def shifted_rows(v, by):
    if by == 0:
        return v
    pad = jnp.zeros((abs(by), v.shape[1]), v.dtype)
    return jnp.concatenate([v[by:], pad], 0) if by > 0 else jnp.concatenate([pad, v[:by]], 0)


def repeated(row):
    return jnp.broadcast_to(row, (SUB16, row.shape[1])).astype(BF)


def numbers(first, width):
    return (lax.broadcasted_iota(jnp.int32, (SUB16, width), 0) + first).astype(F32).astype(BF)


def equal_rows(row, rows):
    wide = repeated(row)
    return [numbers(SUB16 * k, row.shape[1]) == wide for k in range(rows // SUB16)]


def chosen(masks, row):
    wide = repeated(row)
    none = jnp.zeros_like(wide)
    return jnp.concatenate([jnp.where(m, wide, none) for m in masks], 0)


def pack_kernel(dose_hbm, owner_hbm, cell_hbm, offset_hbm, send_ref, rank_ref, owner_ref,
                dose_v, owner_v, cell_v, offset_v, sems):
    copies = [pltpu.make_async_copy(src, dst, sems.at[n]) for n, (src, dst) in enumerate(
        ((owner_hbm, owner_v), (cell_hbm, cell_v), (offset_hbm, offset_v), (dose_hbm, dose_v)))]
    for copy in copies:
        copy.start()
    chunk = 256
    n_chunks = S_DEV // chunk
    rows_at = lax.broadcasted_iota(jnp.int32, (chunk, chunk), 0)
    cols_at = lax.broadcasted_iota(jnp.int32, (chunk, chunk), 1)
    before = jnp.where(rows_at < cols_at, 1.0, 0.0).astype(BF)
    copies[0].wait()
    owner = owner_v[...].astype(F32)
    owner_ref[...] = owner
    mine = equal_rows(owner, N_ROW)
    ones = chosen(mine, jnp.ones((1, S_DEV), F32))
    stacked = jnp.concatenate([ones[:, c * chunk:(c + 1) * chunk] for c in range(n_chunks)], 0)
    prefix = nn_dot(stacked, before)
    totals = prefix[:, chunk - 1:] + stacked[:, chunk - 1:].astype(F32)
    base = jnp.zeros((N_ROW, 1), F32)
    ranks = []
    for c in range(n_chunks):
        here = slice(c * N_ROW, (c + 1) * N_ROW)
        inside = ones[:, c * chunk:(c + 1) * chunk].astype(F32)
        ranks.append(jnp.sum(inside * (prefix[here] + base), axis=0, keepdims=True))
        base = base + totals[here]
    rank = jnp.concatenate(ranks, 1)
    rank_ref[...] = rank
    at_rank = chosen(equal_rows(rank, CAP), jnp.ones((1, S_DEV), F32))
    for copy in copies[1:]:
        copy.wait()
    place = (cell_v[...] * 256 + offset_v[...]).astype(F32)
    dose = dose_v[...]
    parts = [chosen(mine, part) for part in split3(place) + split3(dose)]
    packed = nt_dot(jnp.concatenate(parts, 0), at_rank)
    for which in range(2):
        p = packed[3 * which * N_ROW:3 * (which + 1) * N_ROW]
        whole = p[:N_ROW] + p[N_ROW:2 * N_ROW] + p[2 * N_ROW:]
        for t in range(NT):
            start = (2 * t + which) * CAP
            send_ref[:, 0, start:start + CAP] = shifted_rows(whole, t - REACH)


def decoded(place):
    cell = jnp.floor(place * (1.0 / 256.0))
    fine = place - 256.0 * cell
    cell_y = jnp.floor((cell + 0.5) * (1.0 / (CX - 1)))
    cell_x = cell - (CX - 1) * cell_y
    off_y = jnp.floor(fine * (1.0 / 16.0))
    off_x = fine - 16.0 * off_y
    block = jnp.floor(cell_x * (1.0 / BLK))
    column = cell_x - BLK * block
    off_y, off_x = off_y * (1.0 / 16.0), off_x * (1.0 / 16.0)
    return dict(block=block, y=cell_y, y1=cell_y + 1.0, column=column, column1=column + 1.0,
                y0w=1.0 - off_y, y1w=off_y, x0=1.0 - off_x, x1=off_x)


def pair_columns(shot, i):
    return jnp.concatenate([column_chunk(shot, i), column_chunk(shot, i + 1)], 1)


def over_rows(v, i):
    return jnp.broadcast_to(v[i:i + 1], (SUB16, CAP)).astype(BF)


def row_numbers(first):
    return (lax.broadcasted_iota(jnp.int32, (SUB16, CAP), 0) + first).astype(F32).astype(BF)


def column_chunk(shot, i):
    first, w1 = over_rows(shot["column"], i), over_rows(shot["x1"], i)
    second, w0 = first + jnp.ones_like(first), jnp.ones_like(w1) - w1
    none = jnp.zeros_like(w0)
    out = []
    for k in range(XR // SUB16):
        at = row_numbers(SUB16 * k)
        out.append(jnp.where(at == first, w0, jnp.where(at == second, w1, none)))
    return jnp.concatenate(out, 0)


def row_chunk(shot, dosed, i, at_dosed):
    first = over_rows(shot["y"], i)
    second = first + jnp.ones_like(first)
    block = over_rows(shot["block"], i)
    values = [over_rows(v, at_dosed) for v in dosed]
    none = jnp.zeros_like(first)
    parts = [[], []]
    for k in range(CY // SUB16):
        at = row_numbers(SUB16 * k)
        on_first, on_second = at == first, at == second
        for part in range(2):
            q0, q1 = values[2 * part:2 * part + 2]
            parts[part].append(jnp.where(on_first, q0, jnp.where(on_second, q1, none)))
    inside = [block == jnp.full((SUB16, CAP), h, F32).astype(BF) for h in range(NB)]
    return jnp.concatenate([jnp.where(inside[h], v, none) for part in parts for h in range(NB) for v in part], 0)


def dosed_weights(shot, dose, sources=slice(None)):
    hi0, lo0 = split2(shot["y0w"][sources] * dose)
    hi1, lo1 = split2(shot["y1w"][sources] * dose)
    return [v.astype(F32) for v in (hi0, hi1, lo0, lo1)]


def density_pair(shot, dosed, first, i, columns):
    a = jnp.concatenate([row_chunk(shot, dosed, j, j - first) for j in (i, i + 1)], 1)
    return nt_dot(a, columns)


def assembled(both):
    d = both[:BLK] + both[BLK:]
    blocks = [d[:CY, :BLK]]
    for h in range(1, NB):
        over = d[(h - 1) * CY:h * CY, BLK:XR]
        over = jnp.concatenate([over, jnp.zeros((CY, BLK - XR + BLK), F32)], 1)
        blocks.append(d[h * CY:(h + 1) * CY, :BLK] + over)
    return jnp.concatenate(blocks, 1)


def added(total, one):
    return one if total is None else total + one


def tile_density(shot, dose):
    dosed = dosed_weights(shot, dose)
    both = None
    for i in range(0, N_ROW, 2):
        both = added(both, density_pair(shot, dosed, 0, i, pair_columns(shot, i)))
    return assembled(both)


def packed_edge(block, lane0):
    rows = block.shape[0] // 4
    lane = lax.broadcasted_iota(jnp.int32, (rows, BLK), 1)
    out = jnp.zeros((rows, BLK), block.dtype)
    for g in range(4):
        part = block[g * rows:(g + 1) * rows]
        shift = (32 * g - lane0) % BLK
        part = pltpu.roll(part, shift, 1) if shift else part
        out = jnp.where(lane // 32 == g, part, out)
    return out


def unpacked_edge(edge, lane0):
    parts = []
    for g in range(4):
        shift = (lane0 - 32 * g) % BLK
        parts.append(pltpu.roll(edge, shift, 1) if shift else edge)
    return jnp.concatenate(parts, 0)


def blurred_y(tiles, taps_ref):
    both = None
    for n, density in enumerate(tiles):
        both = added(both, nn_dot(taps_ref[n], jnp.concatenate(split2(density), 0)))
    rows = both.shape[0] // 2
    return both[:rows] + both[rows:]


def edge_products(stacked, taps):
    both = nn_dot(jnp.concatenate(split2(stacked), 0), taps)
    rows = stacked.shape[0]
    both = both[:rows] + both[rows:]
    return both[:, :BLK] + both[:, BLK:]


def blurred_inside(along_y, taps_ref):
    none = jnp.zeros((along_y.shape[0], BLK), F32)
    wide = jnp.concatenate([none, along_y, none], 1)
    rows = along_y.shape[0]
    out = edge_products(jnp.concatenate([wide[:, h * BLK:(h + 3) * BLK] for h in range(NB)], 0), taps_ref[...])
    return jnp.concatenate([out[h * rows:(h + 1) * rows] for h in range(NB)], 1)


def blurred_sides(from_left_ref, from_right_ref, taps_ref):
    col = lax.axis_index("col")
    left = unpacked_edge(jnp.where(col > 0, from_left_ref[...], 0.0), BLK - 32)
    right = unpacked_edge(jnp.where(col < N_COL - 1, from_right_ref[...], 0.0), 0)
    return edge_products(left, taps_ref[:BLK]), edge_products(right, taps_ref[2 * BLK:])


def gather_table(total):
    pieces = []
    for h in range(NB):
        inside = total[:, h * BLK:(h + 1) * BLK]
        if h + 1 < NB:
            after = total[:, (h + 1) * BLK:(h + 1) * BLK + XR - BLK]
        else:
            after = jnp.zeros((CY, XR - BLK), F32)
        pieces.append(jnp.concatenate([inside, after], 1))
    return jnp.concatenate(split2(jnp.concatenate(pieces, 0)), 0)


def gather_pair(table, shot, i, columns):
    both = nn_dot(table, columns)
    at = lax.broadcasted_iota(jnp.int32, (CY, CAP), 0).astype(F32)
    rows = []
    for j in range(2):
        here = slice(j * CAP, (j + 1) * CAP)
        g = both[:BLK, here] + both[BLK:, here]
        block, y, y1, w0, w1 = (shot[name][i + j:i + j + 1] for name in ("block", "y", "y1", "y0w", "y1w"))
        mine = g[:CY]
        for h in range(1, NB):
            mine = jnp.where(block == float(h), g[h * CY:(h + 1) * CY], mine)
        w = jnp.where(at == y, w0, jnp.where(at == y1, w1, 0.0))
        rows.append(jnp.sum(w * mine, axis=0, keepdims=True))
    return rows


def corrected(dose, exposure):
    return jnp.where(dose > 0.0, dose * (1.0 + BACKSCATTER) / exposure, 0.0)


def slots(recv_ref, t):
    start = 2 * t * CAP
    return recv_ref[:, 0, start:start + CAP], recv_ref[:, 0, start + CAP:start + 2 * CAP]


def first_kernel(recv_ref, ltaps_ref, along_ref, density_ref, to_left_ref, to_right_ref):
    tiles = []
    for t in range(NT):
        place, dose = slots(recv_ref, t)
        shot = decoded(place)
        tiles.append(tile_density(shot, dose))
    density_ref[...] = jnp.concatenate(tiles[1:NT - 1], 0)
    along = blurred_y(tiles, ltaps_ref)
    along_ref[...] = along
    to_left_ref[...] = packed_edge(along[:, :BLK], 0)
    to_right_ref[...] = packed_edge(along[:, CX - BLK:], BLK - 32)


def inside_kernel(along_ref, rtaps_ref, field_ref):
    field_ref[...] = blurred_inside(along_ref[...], rtaps_ref)


def full_field(inside_ref, from_left_ref, from_right_ref, rtaps_ref):
    left, right = blurred_sides(from_left_ref, from_right_ref, rtaps_ref)
    return jnp.concatenate(
        [inside_ref[:, :BLK] + left, inside_ref[:, BLK:CX - BLK], inside_ref[:, CX - BLK:] + right], 1)


def second_kernel(recv_ref, inside_ref, density_ref, from_left_ref, from_right_ref, rtaps_ref, ltaps_ref,
                  dose_ref, along2_ref, density2_ref, to_left_ref, to_right_ref, b_ref):
    total = density_ref[...] + BACKSCATTER * full_field(inside_ref, from_left_ref, from_right_ref, rtaps_ref)
    places = [slots(recv_ref, n + 1) for n in range(NT - 2)]
    shots = [decoded(place) for place, _ in places]
    tables = [gather_table(total[n * CY:(n + 1) * CY]) for n in range(NT - 2)]
    densities = [None] * (NT - 2)
    groups = [(n, first) for n in range(NT - 2) for first in range(0, N_ROW, GROUP)]
    dosed = None
    for step in range(len(groups) + 1):
        rows = []
        for j in range(0, GROUP, 2):
            if step < len(groups):
                n, first = groups[step]
                columns = pair_columns(shots[n], first + j)
                b_ref[n, :, (first + j) * CAP:(first + j + 2) * CAP] = columns
                rows += gather_pair(tables[n], shots[n], first + j, columns)
            if step > 0:
                m, start = groups[step - 1]
                columns = b_ref[m, :, (start + j) * CAP:(start + j + 2) * CAP]
                densities[m] = added(densities[m], density_pair(shots[m], dosed, start, start + j, columns))
        if rows:
            sources = slice(first, first + GROUP)
            dose = corrected(places[n][1][sources], jnp.concatenate(rows, 0))
            if n + 1 == REACH:
                dose_ref[sources, :] = dose
            dosed = dosed_weights(shots[n], dose, sources)
    tiles = [assembled(both) for both in densities]
    density2_ref[...] = tiles[1]
    along = blurred_y(tiles, ltaps_ref)
    along2_ref[...] = along
    to_left_ref[...] = packed_edge(along[:, :BLK], 0)
    to_right_ref[...] = packed_edge(along[:, CX - BLK:], BLK - 32)


def third_kernel(recv_ref, dose_ref, inside_ref, density_ref, from_left_ref, from_right_ref, rtaps_ref, field_hbm, final_ref,
                 field_ref, sem):
    field = full_field(inside_ref, from_left_ref, from_right_ref, rtaps_ref)
    field_ref[...] = field
    copy = pltpu.make_async_copy(field_ref, field_hbm, sem)
    copy.start()
    shot = decoded(slots(recv_ref, REACH)[0])
    table = gather_table(density_ref[...] + BACKSCATTER * field)
    rows = []
    for i in range(0, N_ROW, 2):
        rows += gather_pair(table, shot, i, pair_columns(shot, i))
    final_ref[:, 0, :] = corrected(dose_ref[...], jnp.concatenate(rows, 0))
    copy.wait()


def unpack_kernel(ret_ref, owner_ref, rank_ref, out_ref):
    at_rank = chosen(equal_rows(rank_ref[...], CAP), jnp.ones((1, S_DEV), F32))
    parts = jnp.concatenate([p.astype(BF) for p in split3(ret_ref[:, 0, :])], 0)
    g = nn_dot(parts, at_rank)
    whole = g[:N_ROW] + g[N_ROW:2 * N_ROW] + g[2 * N_ROW:]
    mine = owner_ref[...] == lax.broadcasted_iota(jnp.int32, (N_ROW, S_DEV), 0).astype(F32)
    out_ref[...] = jnp.sum(jnp.where(mine, whole, 0.0), axis=0, keepdims=True)


def call(kernel, outs, n_in, scratch=(), space=pltpu.VMEM, out_spaces=None):
    return pl.pallas_call(
        kernel,
        out_shape=[jax.ShapeDtypeStruct(s, F32) for s in outs],
        in_specs=[pl.BlockSpec(memory_space=space)] * n_in,
        out_specs=[pl.BlockSpec(memory_space=s) for s in out_spaces or [pltpu.VMEM] * len(outs)],
        scratch_shapes=list(scratch),
        compiler_params=pltpu.CompilerParams(vmem_limit_bytes=48 << 20),
    )


def exchanged(to_left, to_right):
    n = lax.axis_size("col")
    from_left = lax.ppermute(to_right, "col", [(i, (i + 1) % n) for i in range(n)])
    from_right = lax.ppermute(to_left, "col", [((i + 1) % n, i) for i in range(n)])
    return from_left, from_right


def per_device(shot_dose, shot_owner, shot_cell, shot_offset):
    ltaps = jnp.asarray(left_constant(3 * CY, NT * CY, CY))
    ltaps2 = jnp.asarray(left_constant(CY, 3 * CY, CY))
    rtaps = jnp.asarray(right_constant())
    row = (1, S_DEV)
    rows = [pltpu.VMEM(row, F32)] + [pltpu.VMEM(row, jnp.int32)] * 3 + [pltpu.SemaphoreType.DMA((4,))]
    send, rank, owner = call(pack_kernel, [(N_ROW, 1, 2 * NT * CAP), row, row], 4, rows, pltpu.HBM)(
        *(pltpu.with_memory_space_constraint(v.reshape(row), pltpu.HBM) for v in (shot_dose, shot_owner, shot_cell, shot_offset))
    )
    recv = lax.all_to_all(send, "row", split_axis=0, concat_axis=0, tiled=True)
    edge = (3 * CY // 4, BLK)
    along, density, to_left, to_right = call(first_kernel, [(3 * CY, CX), (3 * CY, CX), edge, edge], 2)(recv, ltaps)
    from_left, from_right = exchanged(to_left, to_right)
    (inside,) = call(inside_kernel, [(3 * CY, CX)], 2)(along, rtaps)
    edge = (CY // 4, BLK)
    dose, along, density, to_left, to_right = call(
        second_kernel, [(N_ROW, CAP), (CY, CX), (CY, CX), edge, edge], 7, (pltpu.VMEM((NT - 2, XR, SLOTS), BF),)
    )(recv, inside, density, from_left, from_right, rtaps, ltaps2)
    from_left, from_right = exchanged(to_left, to_right)
    (inside,) = call(inside_kernel, [(CY, CX)], 2)(along, rtaps)
    field, final = call(
        third_kernel, [(CY, CX), (N_ROW, 1, CAP)], 7, (pltpu.VMEM((CY, CX), F32), pltpu.SemaphoreType.DMA),
        out_spaces=[pltpu.HBM, pltpu.VMEM],
    )(
        recv, dose, inside, density, from_left, from_right, rtaps
    )
    back = lax.all_to_all(final, "row", split_axis=0, concat_axis=0, tiled=True)
    (out,) = call(unpack_kernel, [(1, S_DEV)], 3)(back, owner, rank)
    return out.reshape(S_DEV), field


def solution(mesh):
    placed = (P(("row", "col")), P(("row", "col"), None), P(("row", "col")), P(("row", "col")))
    return jax.shard_map(
        per_device,
        mesh=mesh,
        in_specs=placed,
        out_specs=(P(("row", "col")), P("row", "col")),
        check_vma=False,
    )
```
